256 devices in a mesh: row: 8 (over x, y_lo), col: 32 (over z, y_hi, core).
Axes of the slice: x: 4, y: 4 (y_hi: 2, y_lo: 2; y = y_hi * 2 + y_lo), z: 8, core: 2. Of those that a mesh axis runs over, the one named last changes fastest.
Arguments:
- matrix: bfloat16 [3584, 18432], P('row', 'col'), may hold values from -0.046875 to 0.046875
Outputs:
- update: bfloat16 [3584, 18432], P('row', 'col')
The draws below stay inside these ranges and needn't reach their ends.
All inputs are finite; a program needn't handle non-finite values.
Results may differ from the reference program's by a relative error of at most 0.0092.
Values may be sent and summed in bfloat16 or wider, within the bound.
No kernel may reach another device: no remote copies, remote signals or barrier semaphores. Data moves between devices by JAX's collectives and lax.ppermute only.
A program may use at most 64 MiB of HBM per device.

```python
import math
import jax
import jax.numpy as jnp

M = 3584
N = 18432


def block_levels(own_key, shape, pieces, smallest, high):
    def one(dim, parts):
        steps = jax.random.uniform(jax.random.fold_in(jax.random.fold_in(own_key, 6), dim), (parts,), jnp.float32, smallest / len(pieces), high / len(pieces))
        return jnp.repeat(jnp.exp(steps), shape[dim] // parts).reshape((-1,) + (1,) * (len(shape) - dim - 1))

    level = one(*pieces[0])
    for cut in pieces[1:]:
        level = level * one(*cut)
    return level


def centred(own_key, shape, width, most, shards=(), kind=jnp.bfloat16):
    result = jax.random.normal(own_key, shape, jnp.float32) * width
    if len(shards) > 0:
        result = block_levels(own_key, shape, shards, -0.22, 0.18) * result
    return jnp.clip(result, min=-most, max=most).astype(kind)


def setup_inputs(seed: int = 0) -> dict:
    key_list = jax.random.split(jax.random.key(seed), 2)
    return {
        "matrix": centred(key_list[0], (M, N), N ** -0.5, 0.046875, ((0, 8), (1, 32))),
    }


coef_a = 3.4445
coef_b = -4.775
coef_c = 2.0315

def reference(matrix):
    gram_full = jnp.dot(matrix, matrix.T, preferred_element_type=jnp.float32).astype(jnp.bfloat16)
    square = jnp.dot(gram_full, gram_full, preferred_element_type=jnp.float32)
    poly_full = (coef_b * gram_full.astype(jnp.float32) + coef_c * square).astype(jnp.bfloat16)
    product = jnp.dot(poly_full, matrix, preferred_element_type=jnp.float32)
    factor = 0.2 * math.sqrt(max(M, N))
    return ((coef_a * matrix.astype(jnp.float32) + product) * factor).astype(jnp.bfloat16)
```

```python
import itertools
import math

import jax
import jax.numpy as jnp
import numpy as np
from jax import lax
from jax.sharding import Mesh
from jax.sharding import PartitionSpec as P

coef_a = 3.4445
coef_b = -4.775
coef_c = 2.0315


SIZES = {"x": 4, "yl": 2, "z": 8, "yh": 2, "c": 2}
AXES = tuple(SIZES)
ROW = ("x", "yl")
COL = ("z", "yh", "c")


def shift(value, axis, step):
    size = SIZES[axis]
    return lax.ppermute(value, axis, [((i + step) % size, i) for i in range(size)])


def gather_panel(own, use):
    half = own.shape[0] // 2
    got = {(0, 0): own}

    def put(key, value):
        got[key] = value
        use(key, value)

    use((0, 0), own)
    first = shift(own, "x", 1), shift(own, "x", -1), shift(own, "yl", 1)
    put((1, 0), first[0])
    put((3, 0), first[1])
    put((0, 1), first[2])
    r10, r30, r01 = first
    up = jnp.concatenate([r10[:half], r01[:half]], 0)
    down = jnp.concatenate([r30[half:], r01[:half]], 0)
    side = jnp.concatenate([r10[half:], r30[half:]], 0)
    up, down, side = shift(up, "x", 1), shift(down, "x", -1), shift(side, "yl", 1)
    r20 = jnp.concatenate([up[:half], down[:half]], 0)
    r11 = jnp.concatenate([up[half:], side[:half]], 0)
    r31 = jnp.concatenate([down[half:], side[half:]], 0)
    put((2, 0), r20)
    put((1, 1), r11)
    put((3, 1), r31)
    a, b = 160, 304
    last = shift(r11[:a], "x", 1), shift(r31[a:b], "x", -1), shift(r20[b:], "yl", 1)
    put((2, 1), jnp.concatenate(last, 0))
    return got


ORDER = [(0, 0), (1, 0), (3, 0), (0, 1), (2, 0), (1, 1), (3, 1), (2, 1)]


def on_device(matrix):
    rows, cols = matrix.shape
    z, yh, c = (lax.axis_index(n) for n in COL)
    full_rows = rows * 8
    parts = {}

    def gram(key, block):
        parts[key] = lax.dot_general(
            matrix, block, (((1,), (1,)), ((), ())), preferred_element_type=jnp.float32
        ).astype(jnp.bfloat16)

    panel = gather_panel(matrix, gram)
    lower = jnp.concatenate([parts[k] for k in ORDER[:4]], 1)
    upper = jnp.concatenate([parts[k] for k in ORDER[4:]], 1)
    keep = jnp.where(c == 0, lower, upper)
    send = jnp.where(c == 0, upper, lower)
    pair = (keep.astype(jnp.float32) + shift(send, "c", 1).astype(jnp.float32)).astype(jnp.bfloat16)
    half = pair.shape[1] // 2
    stacked = jnp.stack([pair[:, :half], pair[:, half:]], 0).reshape(2, 8, rows // 8, half)
    stacked = stacked.reshape(16, rows // 8, half)
    pieces = lax.all_to_all(stacked, ("yh", "z"), 0, 0, tiled=True)
    piece = jnp.sum(pieces.astype(jnp.float32), 0).astype(jnp.bfloat16)
    other = shift(piece, "yh", 1)
    piece = jnp.where(yh == 0, jnp.concatenate([piece, other], 1), jnp.concatenate([other, piece], 1))
    ring = {0: piece}
    up, down = piece, piece
    for step in range(1, 4):
        up, down = shift(up, "z", 1), shift(down, "z", -1)
        ring[step], ring[8 - step] = up, down
    w = piece.shape[1] // 2
    ring[4] = jnp.concatenate([shift(up[:, :w], "z", 1), shift(down[:, w:], "z", -1)], 1)
    chain = jnp.concatenate([ring[i] for i in range(8)] * 2, 0)
    mine = lax.dynamic_slice_in_dim(chain, ((8 - z) % 8) * (rows // 8), rows, 0)
    theirs = shift(mine, "c", 1)
    gram_row = jnp.where(c == 0, jnp.concatenate([mine, theirs], 1), jnp.concatenate([theirs, mine], 1))
    blocks = {k: gram_row[:, i * rows : (i + 1) * rows] for i, k in enumerate(ORDER)}

    x_panel = jnp.concatenate([panel[k] for k in ORDER], 0)
    y = jnp.dot(gram_row, x_panel, preferred_element_type=jnp.float32)
    w32 = coef_b * matrix.astype(jnp.float32) + coef_c * y
    w_high = w32.astype(jnp.bfloat16)
    w_low = (w32 - w_high.astype(jnp.float32)).astype(jnp.bfloat16)
    total = [coef_a * matrix.astype(jnp.float32) + jnp.dot(blocks[(0, 0)], w_low, preferred_element_type=jnp.float32)]

    def add(key, block):
        total[0] = total[0] + jnp.dot(blocks[key], block, preferred_element_type=jnp.float32)

    gather_panel(w_high, add)
    factor = 0.2 * math.sqrt(max(full_rows, cols * 32))
    return (total[0] * factor).astype(jnp.bfloat16)


def solution(mesh):
    fine = Mesh(mesh.devices.reshape(tuple(SIZES.values())), AXES)
    return jax.shard_map(on_device, mesh=fine, in_specs=(P(ROW, COL),), out_specs=P(ROW, COL), check_vma=False)
```

```python
import math

import jax
import jax.numpy as jnp
from jax import lax
from jax.experimental import pallas as pl
from jax.experimental.pallas import tpu as pltpu
from jax.sharding import Mesh
from jax.sharding import PartitionSpec as P

coef_a = 3.4445
coef_b = -4.775
coef_c = 2.0315


SIZES = {"x": 4, "yl": 2, "z": 8, "yh": 2, "c": 2}
AXES = tuple(SIZES)
ROW = ("x", "yl")
COL = ("z", "yh", "c")
RING = SIZES["z"]
PANEL = SIZES["x"] * SIZES["yl"]

F32 = jnp.float32
BF16 = jnp.bfloat16
VMEM = pl.BlockSpec(memory_space=pltpu.VMEM)
SMEM = pl.BlockSpec(memory_space=pltpu.SMEM)


def shift(value, axis, step):
    size = SIZES[axis]
    return lax.ppermute(value, axis, [((i + step) % size, i) for i in range(size)])


def call(body, name, place, operands, outs, scratch=()):
    return pl.pallas_call(
        body,
        name=name,
        out_shape=outs,
        in_specs=[SMEM] + [VMEM] * len(operands),
        out_specs=jax.tree.map(lambda _: VMEM, outs),
        scratch_shapes=list(scratch),
    )(place, *operands)


def first_blocks(own):
    return own, shift(own, "x", 1), shift(own, "x", -1), shift(own, "yl", 1)


def more_blocks(first):
    _, r10, r30, r01 = first
    return shift(r30, "x", -1), shift(r01, "x", 1), shift(r30, "yl", 1)


def last_block(more):
    r20, r11, r31 = more
    a, b = 144, 288
    return shift(r11[:a], "x", 1), shift(r31[a:b], "x", -1), shift(r20[b:], "yl", 1)


def fill(panel, refs):
    half = panel.shape[1]
    at = 0
    for ref in refs:
        size = ref.shape[0]
        panel[at // half, pl.ds(at % half, size), :] = ref[...]
        at += size


def gram_body(place, own, *refs):
    *blocks, keep, send, panel = refs
    fill(panel, blocks)
    z, c = place[0], place[1]
    dims = (((1,), (1,)), ((), ()))
    left = lax.dot_general(own[...], panel[0], dims, preferred_element_type=F32)
    right = lax.dot_general(own[...], panel[1], dims, preferred_element_type=F32)
    kept = jnp.where(c == 0, left, right).astype(BF16)
    sent = jnp.where(c == 0, right, left).astype(BF16)
    size = keep.shape[1]
    for chunk in range(RING):
        at = lax.rem(chunk - z + RING, RING)
        keep[at] = kept[chunk * size : (chunk + 1) * size]
        send[at] = sent[chunk * size : (chunk + 1) * size]


def gram_partial(place, own, blocks, name):
    rows, cols = own.shape
    part = jax.ShapeDtypeStruct((RING, rows // RING, 2 * rows), BF16)
    panel = jax.ShapeDtypeStruct((2, 2 * rows, cols), BF16)
    return call(gram_body, name, place, (own, *blocks), [part, part, panel])


def add(a, b):
    return (a.astype(F32) + b.astype(F32)).astype(BF16)


def ring_sum(part):
    cut = 512
    up, down = part[4][:, :cut], part[4][:, cut:]
    for step in range(3, -1, -1):
        up, down = shift(up, "z", -1), shift(down, "z", 1)
        if step == 0:
            total = part[0].astype(F32) + up.astype(F32) + down.astype(F32)
        elif step == 3:
            up = jnp.concatenate([add(part[3][:, :cut], up), part[3][:, cut:]], 1)
            down = jnp.concatenate([part[5][:, :cut], add(part[5][:, cut:], down)], 1)
        else:
            up, down = add(part[step], up), add(part[RING - step], down)
    return total.astype(BF16)


def update_body(place, own, low, high, *refs):
    *pieces, near, far, w_high, w_low = refs
    z, c = place[0], place[1]
    size = near.shape[1] // RING
    count = len(pieces) // 2
    for side, group in ((c, pieces[:count]), (1 - c, pieces[count:])):
        for d in range(RING):
            at = pl.ds(pl.multiple_of(lax.rem(z + d, RING) * size, 8), size)
            if d == RING // 2:
                lower, upper = group[d][...], group[d + 1][...]
            else:
                ref = group[d if d < RING // 2 else d + 1]
                lower, upper = ref[:size], ref[size:]
            near[side, at, :] = lower
            far[side, at, :] = upper
    total = jnp.zeros(own.shape, F32)
    for gram, panel in ((near, low), (far, high)):
        for i in range(2):
            total += jnp.dot(gram[i], panel[i], preferred_element_type=F32)
    w = coef_b * own[...].astype(F32) + coef_c * total
    top = w.astype(BF16)
    w_high[...] = top
    w_low[...] = (w - top.astype(F32)).astype(BF16)


def near_body(place, own, w_low, gram, *refs):
    *blocks, total, panel = refs
    rows = own.shape[0]
    fill(panel, blocks)
    acc = coef_a * own[...].astype(F32)
    acc += jnp.dot(gram[0][:, :rows], w_low[...], preferred_element_type=F32)
    acc += jnp.dot(gram[0], panel[0], preferred_element_type=F32)
    total[...] = acc + jnp.dot(gram[1], panel[1], preferred_element_type=F32)


def side_body(place, before, gram, *refs):
    *blocks, total, panel = refs
    fill(panel, blocks)
    total[...] = before[...] + jnp.dot(gram[0], panel[0], preferred_element_type=F32)


def far_body(place, before, gram, *refs):
    *blocks, out, panel = refs
    fill(panel, blocks)
    acc = before[...] + jnp.dot(gram[1], panel[0], preferred_element_type=F32)
    out[...] = (acc * out_scale(out)).astype(BF16)


def out_scale(out):
    return 0.2 * math.sqrt(max(out.shape[0] * PANEL, out.shape[1] * SIZES["z"] * SIZES["yh"] * SIZES["c"]))


def on_device(matrix):
    rows, cols = matrix.shape
    place = jnp.stack([lax.axis_index("z"), lax.axis_index("c")]).astype(jnp.int32)

    first = first_blocks(matrix)
    keep, send, low = gram_partial(place, matrix, first, "gram_low")
    sums = [ring_sum(add(keep, shift(send, "c", 1)))]
    more = more_blocks(first)
    last = last_block(more)
    keep, send, high = gram_partial(place, matrix, (*more, *last), "gram_high")
    sums.append(ring_sum(add(keep, shift(send, "c", 1))))
    mine = jnp.concatenate(sums, 0)
    mine = add(mine, shift(mine, "yh", 1))

    size = rows // RING
    ring = {0: mine}
    up, down = mine, mine
    for step in range(1, RING // 2):
        up, down = shift(up, "z", 1), shift(down, "z", -1)
        ring[step], ring[RING - step] = up, down
    middle = [shift(up[:size], "z", 1), shift(down[size:], "z", -1)]
    pieces = [ring[d] for d in range(RING // 2)] + middle + [ring[d] for d in range(RING // 2 + 1, RING)]
    others = [shift(p, "c", 1) for p in pieces]

    block = jax.ShapeDtypeStruct((rows, cols), BF16)
    wide = jax.ShapeDtypeStruct((2, rows, 2 * rows), BF16)
    gram_near, gram_far, w_high, w_low = call(
        update_body, "update", place, (matrix, low, high, *pieces, *others), [wide, wide, block, block]
    )
    sums = jax.ShapeDtypeStruct((rows, cols), F32)
    panel = pltpu.VMEM((1, 2 * rows, cols), BF16)
    near = first_blocks(w_high)
    total = call(
        near_body,
        "near",
        place,
        (matrix, w_low, gram_near, *near),
        sums,
        [pltpu.VMEM((2, 2 * rows, cols), BF16)],
    )
    side = more_blocks(near)
    total = call(side_body, "side", place, (total, gram_far, *side[:2]), sums, [panel])
    return call(far_body, "far", place, (total, gram_far, side[2], *last_block(side)), block, [panel])


def solution(mesh):
    fine = Mesh(mesh.devices.reshape(tuple(SIZES.values())), AXES)
    return jax.shard_map(on_device, mesh=fine, in_specs=(P(ROW, COL),), out_specs=P(ROW, COL), check_vma=False)
```

```python
import math

import jax
import jax.numpy as jnp
from jax import lax
from jax.experimental import pallas as pl
from jax.experimental.pallas import tpu as pltpu
from jax.sharding import Mesh
from jax.sharding import PartitionSpec as P

coef_a = 3.4445
coef_b = -4.775
coef_c = 2.0315


SIZES = {"x": 4, "yl": 2, "z": 8, "yh": 2, "c": 2}
AXES = tuple(SIZES)
ROW = ("x", "yl")
COL = ("z", "yh", "c")
RING = SIZES["z"]
PANEL = SIZES["x"] * SIZES["yl"]

VMEM_LIMIT = 20 << 20

F32 = jnp.float32
BF16 = jnp.bfloat16
VMEM = pl.BlockSpec(memory_space=pltpu.VMEM)
SMEM = pl.BlockSpec(memory_space=pltpu.SMEM)


def shift(value, axis, step):
    size = SIZES[axis]
    return lax.ppermute(value, axis, [((i + step) % size, i) for i in range(size)])


def call(body, name, place, operands, outs, flops=0, scratch=()):
    operands = [pltpu.with_memory_space_constraint(a, pltpu.VMEM) for a in operands]
    single = not isinstance(outs, list)
    outs = [outs] if single else outs
    moved = sum(math.prod(a.shape) * 2 for a in (*operands, *outs))
    got = pl.pallas_call(
        body,
        name=name,
        out_shape=[pltpu.VMEM(o.shape, o.dtype) for o in outs],
        in_specs=[SMEM] + [VMEM] * len(operands),
        out_specs=[VMEM] * len(outs),
        scratch_shapes=list(scratch),
        cost_estimate=pl.CostEstimate(flops=flops, bytes_accessed=moved, transcendentals=0),
        compiler_params=pltpu.CompilerParams(vmem_limit_bytes=VMEM_LIMIT),
    )(place, *operands)
    return got[0] if single else got


def first_blocks(own):
    return own, shift(own, "x", 1), shift(own, "x", -1), shift(own, "yl", 1)


def more_blocks(first):
    _, r10, r30, r01 = first
    return shift(r30, "x", -1), shift(r01, "x", 1), shift(r30, "yl", 1)


def last_block(more):
    _, r11, r31 = more
    half = r11.shape[0] // 2
    return shift(r11[:half], "x", 1), shift(r31[half:], "x", -1)


def fill(panel, refs):
    half = panel.shape[1]
    at = 0
    for ref in refs:
        size = ref.shape[0]
        panel[at // half, pl.ds(at % half, size), :] = ref[...]
        at += size


def gram_body(place, own, *refs):
    *blocks, keep, send, panel = refs
    fill(panel, blocks)
    z, c = place[0], place[1]
    dims = (((1,), (1,)), ((), ()))
    left = lax.dot_general(own[...], panel[0], dims, preferred_element_type=F32)
    right = lax.dot_general(own[...], panel[1], dims, preferred_element_type=F32)
    kept = jnp.where(c == 0, left, right).astype(BF16)
    sent = jnp.where(c == 0, right, left).astype(BF16)
    size = keep.shape[1]
    for chunk in range(RING):
        at = lax.rem(chunk - z + RING, RING)
        keep[at] = kept[chunk * size : (chunk + 1) * size]
        send[at] = sent[chunk * size : (chunk + 1) * size]


def gram_partial(place, own, blocks, name):
    rows, cols = own.shape
    part = jax.ShapeDtypeStruct((RING, rows // RING, 2 * rows), BF16)
    panel = jax.ShapeDtypeStruct((2, 2 * rows, cols), BF16)
    return call(gram_body, name, place, (own, *blocks), [part, part, panel], 8 * rows * rows * cols)


def pair_body(place, low, low_other, high, high_other, *outs):
    size = low.shape[1]
    for d in range(RING):
        lower = (low[d].astype(F32) + low_other[d].astype(F32)).astype(BF16)
        upper = (high[d].astype(F32) + high_other[d].astype(F32)).astype(BF16)
        if d == RING // 2:
            outs[d][...] = lower
            outs[d + 1][...] = upper
        else:
            out = outs[d if d < RING // 2 else d + 1]
            out[:size] = lower
            out[size:] = upper


def add(a, b):
    return (a.astype(F32) + b.astype(F32)).astype(BF16)


def ring_sum(part, up, down):
    size = up.shape[0]
    for step in range(RING // 2 - 1, -1, -1):
        up, down = shift(up, "z", -1), shift(down, "z", 1)
        if step == 0:
            total = part[0].astype(F32) + up.astype(F32) + down.astype(F32)
        elif step == RING // 2 - 1:
            one, two = part[step], part[RING - step]
            up = jnp.concatenate([add(one[:size], up), one[size:]], 0)
            down = jnp.concatenate([two[:size], add(two[size:], down)], 0)
        else:
            up, down = add(part[step], up), add(part[RING - step], down)
    return total.astype(BF16)


def pack_body(place, *refs):
    *pieces, out = refs
    for i, ref in enumerate(pieces):
        out[i] = ref[...]


def update_body(place, own, low, high, own_pack, own_low, own_high, pack, pack_low, pack_high, *refs):
    near, far, w_high, w_low = refs
    z, c = place[0], place[1]
    size = near.shape[1] // RING
    for side, group, group_low, group_high in (
        (c, own_pack, own_low, own_high),
        (1 - c, pack, pack_low, pack_high),
    ):
        for d in range(RING):
            at = pl.ds(pl.multiple_of(lax.rem(z + d, RING) * size, 8), size)
            if d == RING // 2:
                lower, upper = group_low[...], group_high[...]
            else:
                i = d if d < RING // 2 else d - 1
                lower, upper = group[i, :size], group[i, size:]
            near[side, at, :] = lower
            far[side, at, :] = upper
    total = jnp.zeros(own.shape, F32)
    for gram, panel in ((near, low), (far, high)):
        for i in range(2):
            total += jnp.dot(gram[i], panel[i], preferred_element_type=F32)
    w = coef_b * own[...].astype(F32) + coef_c * total
    top = w.astype(BF16)
    w_high[...] = top
    w_low[...] = (w - top.astype(F32)).astype(BF16)


def near_body(place, own, w_low, gram, *refs):
    *blocks, total, panel = refs
    rows = own.shape[0]
    fill(panel, blocks)
    acc = coef_a * own[...].astype(F32)
    acc += jnp.dot(gram[0][:, :rows], w_low[...], preferred_element_type=F32)
    acc += jnp.dot(gram[0], panel[0], preferred_element_type=F32)
    total[...] = acc + jnp.dot(gram[1], panel[1], preferred_element_type=F32)


def side_body(place, before, gram, *refs):
    *blocks, total, panel = refs
    fill(panel, blocks)
    total[...] = before[...] + jnp.dot(gram[0], panel[0], preferred_element_type=F32)


def far_body(place, before, gram, *refs):
    *blocks, out, panel = refs
    fill(panel, blocks)
    acc = before[...] + jnp.dot(gram[1], panel[0], preferred_element_type=F32)
    out[...] = (acc * out_scale(out)).astype(BF16)


def out_scale(out):
    return 0.2 * math.sqrt(max(out.shape[0] * PANEL, out.shape[1] * SIZES["z"] * SIZES["yh"] * SIZES["c"]))


def on_device(matrix):
    rows, cols = matrix.shape
    place = jnp.stack([lax.axis_index("z"), lax.axis_index("c")]).astype(jnp.int32)

    first = lax.optimization_barrier(first_blocks(matrix))
    keep, send, low = gram_partial(place, matrix, first, "gram_low")
    halves = [keep, shift(send, "c", 1)]
    more = lax.optimization_barrier(more_blocks(first))
    last = last_block(more)
    keep, send, high = gram_partial(place, matrix, (*more, *last), "gram_high")
    halves += [keep, shift(send, "c", 1)]
    size = rows // RING
    small = jax.ShapeDtypeStruct((size, 2 * rows), BF16)
    large = jax.ShapeDtypeStruct((2 * size, 2 * rows), BF16)
    middle = RING // 2
    parts = call(pair_body, "pair", place, halves, [large] * middle + [small] * 2 + [large] * (middle - 1))
    part = {d: parts[d if d < middle else d + 1] for d in range(RING) if d != middle}
    mine = ring_sum(part, parts[middle], parts[middle + 1])
    mine = add(mine, shift(mine, "yh", 1))

    ring = {0: mine}
    up, down = mine, mine
    for step in range(1, middle):
        up, down = shift(up, "z", 1), shift(down, "z", -1)
        ring[step], ring[RING - step] = up, down
    far = [shift(up[:size], "z", 1), shift(down[size:], "z", -1)]
    pieces = [ring[d] for d in range(RING) if d != middle]
    packed = jax.ShapeDtypeStruct((RING - 1, 2 * size, 2 * rows), BF16)
    mine = [call(pack_body, "pack", place, pieces, packed), *far]
    mine += [shift(p, "c", 1) for p in mine]

    block = jax.ShapeDtypeStruct((rows, cols), BF16)
    wide = jax.ShapeDtypeStruct((2, rows, 2 * rows), BF16)
    work = 4 * rows * rows * cols
    gram_near, gram_far, w_high, w_low = call(
        update_body, "update", place, (matrix, low, high, *mine), [wide, wide, block, block], 4 * work
    )
    sums = jax.ShapeDtypeStruct((rows, cols), F32)

    def panel(count):
        return [pltpu.VMEM((count, 2 * rows, cols), BF16)]

    near = lax.optimization_barrier(first_blocks(w_high))
    total = call(near_body, "near", place, (matrix, w_low, gram_near, *near), sums, 5 * work // 2, panel(2))
    side = lax.optimization_barrier(more_blocks(near))
    total = call(side_body, "side", place, (total, gram_far, *side[:2]), sums, work, panel(1))
    ends = last_block(side)
    return call(far_body, "far", place, (total, gram_far, side[2], *ends), block, work, panel(1))


def solution(mesh):
    fine = Mesh(mesh.devices.reshape(tuple(SIZES.values())), AXES)
    return jax.shard_map(on_device, mesh=fine, in_specs=(P(ROW, COL),), out_specs=P(ROW, COL), check_vma=False)
```

```python
import math

import jax
import jax.numpy as jnp
from jax import lax
from jax.experimental import pallas as pl
from jax.experimental.pallas import tpu as pltpu
from jax.sharding import Mesh
from jax.sharding import PartitionSpec as P

coef_a = 3.4445
coef_b = -4.775
coef_c = 2.0315


SIZES = {"x": 4, "yl": 2, "z": 8, "yh": 2, "c": 2}
AXES = tuple(SIZES)
ROW = ("x", "yl")
COL = ("z", "yh", "c")
RING = SIZES["z"]
PANEL = SIZES["x"] * SIZES["yl"]
FAR = RING // 2
LANES = 128
VMEM_LIMIT = 20 << 20

F32 = jnp.float32
BF16 = jnp.bfloat16
VMEM = pl.BlockSpec(memory_space=pltpu.VMEM)
SMEM = pl.BlockSpec(memory_space=pltpu.SMEM)


def array(shape, kind=BF16):
    return jax.ShapeDtypeStruct(shape, kind)


def shift(value, axis, step):
    size = SIZES[axis]
    return lax.ppermute(value, axis, [((i + step) % size, i) for i in range(size)])


def ring_shift(value, step):
    pairs = []
    for z in range(RING):
        for c in range(2):
            source = (z + (step if c == 0 else -step)) % RING
            pairs.append((source * 2 + c, z * 2 + c))
    return lax.ppermute(value, ("z", "c"), pairs)


def call(body, name, place, operands, outs, flops=0, scratch=(), fixed=True):
    if fixed:
        operands = [pltpu.with_memory_space_constraint(a, pltpu.VMEM) for a in operands]
    single = not isinstance(outs, list)
    outs = [outs] if single else outs
    moved = sum(math.prod(a.shape) * 2 for a in (*operands, *outs))
    got = pl.pallas_call(
        body,
        name=name,
        out_shape=[pltpu.VMEM(o.shape, o.dtype) for o in outs],
        in_specs=[SMEM] + [VMEM] * len(operands),
        out_specs=[VMEM] * len(outs),
        scratch_shapes=list(scratch),
        cost_estimate=pl.CostEstimate(flops=flops, bytes_accessed=moved, transcendentals=0),
        compiler_params=pltpu.CompilerParams(vmem_limit_bytes=VMEM_LIMIT),
    )(place, *operands)
    return got[0] if single else got


def first_blocks(own):
    return own, shift(own, "x", 1), shift(own, "x", -1), shift(own, "yl", 1)


def more_blocks(first):
    _, r10, r30, r01 = first
    return shift(r30, "x", -1), shift(r01, "x", 1), shift(r30, "yl", 1)


def last_block(more):
    _, r11, r31 = more
    half = (r11.shape[0] // 2 + 15) // 16 * 16
    return shift(r11[:half], "x", 1), shift(r31[half:], "x", -1)


def packing(rows, cols):
    width = cols // LANES * LANES
    rest = cols - width
    groups = width // rest
    return width, rest, groups, rows // groups


def pack(block, out):
    rows, cols = block.shape
    width, rest, groups, height = packing(rows, cols)
    out[:rows] = block[:, :width].astype(BF16)
    for g in range(groups):
        out[rows:, g * rest : (g + 1) * rest] = block[g * height : (g + 1) * height, width:].astype(BF16)


def fill(panel, refs):
    half, cols = panel.shape[1:]
    rows = half // 2
    width, rest, groups, height = packing(rows, cols)
    total = rows + height
    at = 0
    for ref in refs:
        size = ref.shape[0]
        block, begin = divmod(at, total)
        i, base = divmod(block * rows, half)
        main = min(size, rows - begin)
        panel[i, base + begin : base + begin + main, :width] = ref[:main]
        if begin + size == total:
            for g in range(groups):
                low = base + g * height
                panel[i, low : low + height, width:] = ref[main:, g * rest : (g + 1) * rest]
        at += size


def pack_body(place, own, packed, copy):
    value = own[...]
    copy[...] = value
    pack(value.astype(F32), packed)


def stream_row(z, role, far, size):
    to = lax.rem(z + jnp.where(role == 0, far, RING - far), RING)
    return pl.ds(pl.multiple_of(to * size, 8), size)


def gram_body(place, own, *refs):
    *blocks, keep, send, panel, rows = refs
    fill(panel, blocks)
    z, c = place[0], place[1]
    dims = (((1,), (1,)), ((), ()))
    for i in range(2):
        rows[i] = lax.dot_general(own[...], panel[i], dims, preferred_element_type=F32)
    size = keep.shape[1]
    for role, out in ((c, keep), (1 - c, send)):
        units = [(0, role), (FAR, role)]
        for far in range(1, FAR):
            units += [(far, role), (far, 1 - role)]
        for i, (far, side) in enumerate(units):
            out[i] = rows[side, stream_row(z, role, far, size), :].astype(BF16)


def gram_partial(place, own, blocks, name):
    rows, cols = own.shape
    part = array((RING, rows // RING, 2 * rows))
    panel = array((2, 2 * rows, cols))
    scratch = [pltpu.VMEM((2, rows, 2 * rows), F32)]
    return call(gram_body, name, place, (own, *blocks), [part, part, panel], 8 * rows * rows * cols, scratch)


def pair_body(place, low, low_other, high, high_other, near, end, *rest):
    def total(i):
        return [(a[i].astype(F32) + b[i].astype(F32)).astype(BF16) for a, b in ((low, low_other), (high, high_other))]

    for i, out in ((0, near), (1, end)):
        out[0], out[1] = total(i)
    for far, out in enumerate(rest):
        out[0], out[1] = total(2 * far + 2)
        out[2], out[3] = total(2 * far + 3)


def add(a, b):
    return (a.astype(F32) + b.astype(F32)).astype(BF16)


def update_body(place, own, low, high, base, packed, packed_other, end, end_other, *refs):
    near, far, w_high, w_low = refs
    z, c = place[0], place[1]
    size = near.shape[1] // RING

    def put(unit, side, value, where):
        to = near if unit % 2 == 0 else far
        to[side if unit < 2 else 1 - side, where, :] = value

    for unit in range(4):
        put(unit, c, base[unit], stream_row(z, c, 0, size))
    for role, group, tail in ((c, packed, end), (1 - c, packed_other, end_other)):
        for unit in range(2):
            put(unit, role, tail[unit], stream_row(z, role, FAR, size))
        for i in range(FAR - 1):
            for unit in range(4):
                put(unit, role, group[i, unit], stream_row(z, role, i + 1, size))
    total = jnp.zeros(own.shape, F32)
    for gram, panel in ((near, low), (far, high)):
        for i in range(2):
            total += jnp.dot(gram[i], panel[i], preferred_element_type=F32)
    w = coef_b * own[...].astype(F32) + coef_c * total
    pack(w, w_high)
    w_low[...] = (w - w.astype(BF16).astype(F32)).astype(BF16)


def group_body(place, *refs):
    *pieces, out = refs
    for i, ref in enumerate(pieces):
        out[i] = ref[...]


def near_body(place, own, w_low, gram, *refs):
    *blocks, total, panel = refs
    rows = own.shape[0]
    fill(panel, blocks)
    acc = coef_a * own[...].astype(F32)
    acc += jnp.dot(gram[0][:, :rows], w_low[...], preferred_element_type=F32)
    acc += jnp.dot(gram[0], panel[0], preferred_element_type=F32)
    total[...] = acc + jnp.dot(gram[1], panel[1], preferred_element_type=F32)


def side_body(place, before, gram, *refs):
    *blocks, total, panel = refs
    fill(panel, blocks)
    total[...] = before[...] + jnp.dot(gram[0], panel[0], preferred_element_type=F32)


def far_body(place, before, gram, *refs):
    *blocks, out, panel = refs
    fill(panel, blocks)
    acc = before[...] + jnp.dot(gram[1], panel[0], preferred_element_type=F32)
    rows, cols = out.shape
    factor = 0.2 * math.sqrt(max(rows * PANEL, cols * math.prod(SIZES[n] for n in COL)))
    out[...] = (acc * factor).astype(BF16)


def on_device(matrix):
    rows, cols = matrix.shape
    size = rows // RING
    place = jnp.stack([lax.axis_index("z"), lax.axis_index("c")]).astype(jnp.int32)
    width, _, _, height = packing(rows, cols)
    flat = array((rows + height, width))
    block = array((rows, cols))

    packed, own = call(pack_body, "pack", place, (matrix,), [flat, block], fixed=False)
    first = lax.optimization_barrier(first_blocks(packed))
    keep, send, low = gram_partial(place, own, first, "gram_low")
    halves = [keep, shift(send, "c", 1)]
    more = lax.optimization_barrier(more_blocks(first))
    last = last_block(more)
    keep, send, high = gram_partial(place, own, (*more, *last), "gram_high")
    halves += [keep, shift(send, "c", 1)]

    two, four = array((2, size, 2 * rows)), array((4, size, 2 * rows))
    near, end, *rest = call(pair_body, "pair", place, halves, [two, two] + [four] * (FAR - 1))
    moving = ring_shift(end, -1)
    for far in range(FAR - 1, 0, -1):
        mine = rest[far - 1]
        if far == FAR - 1:
            moving = jnp.concatenate([add(mine[:2], moving), mine[2:]], 0)
        else:
            moving = add(mine, moving)
        moving = ring_shift(moving, -1)
    other = shift(moving[2:], "c", 1)
    mine = (near.astype(F32) + moving[:2].astype(F32) + other.astype(F32)).astype(BF16)
    mine = add(mine, shift(mine, "yh", 1))

    base = jnp.concatenate([mine, shift(mine, "c", 1)], 0)
    arrived = [base]
    for _ in range(1, FAR):
        arrived.append(ring_shift(arrived[-1], 1))
    end = ring_shift(arrived[-1][:2], 1)
    group = call(group_body, "group", place, arrived[1:], array((FAR - 1, 4, size, 2 * rows)))
    pieces = [base, group, shift(group, "c", 1), end, shift(end, "c", 1)]

    wide = array((2, rows, 2 * rows))
    work = 4 * rows * rows * cols
    gram_near, gram_far, w_high, w_low = call(
        update_body, "update", place, (own, low, high, *pieces), [wide, wide, flat, block], 4 * work
    )
    sums = array((rows, cols), F32)

    def panel(count):
        return [pltpu.VMEM((count, 2 * rows, cols), BF16)]

    near = lax.optimization_barrier(first_blocks(w_high))
    total = call(near_body, "near", place, (own, w_low, gram_near, *near), sums, 5 * work // 2, panel(2))
    side = lax.optimization_barrier(more_blocks(near))
    total = call(side_body, "side", place, (total, gram_far, *side[:2]), sums, work, panel(1))
    ends = last_block(side)
    return call(far_body, "far", place, (total, gram_far, side[2], *ends), block, work, panel(1))


def solution(mesh):
    fine = Mesh(mesh.devices.reshape(tuple(SIZES.values())), AXES)
    return jax.shard_map(on_device, mesh=fine, in_specs=(P(ROW, COL),), out_specs=P(ROW, COL), check_vma=False)
```

```python
import math

import jax
import jax.numpy as jnp
from jax import lax
from jax.experimental import pallas as pl
from jax.experimental.pallas import tpu as pltpu
from jax.sharding import Mesh
from jax.sharding import PartitionSpec as P


coef_a = 3.4445
coef_b = -4.775
coef_c = 2.0315


SIZES = {"x": 4, "yl": 2, "z": 8, "yh": 2, "c": 2}
AXES = tuple(SIZES)
ROW = ("x", "yl")
COL = ("z", "yh", "c")
RING = SIZES["z"]
PANEL = SIZES["x"] * SIZES["yl"]
FAR = RING // 2
LANES = 128
VMEM_LIMIT = 20 << 20

F32 = jnp.float32
BF16 = jnp.bfloat16
VMEM = pl.BlockSpec(memory_space=pltpu.VMEM)
SMEM = pl.BlockSpec(memory_space=pltpu.SMEM)


def array(shape, kind=BF16):
    return jax.ShapeDtypeStruct(shape, kind)


def shift(value, axis, step):
    size = SIZES[axis]
    return lax.ppermute(value, axis, [((i + step) % size, i) for i in range(size)])


def call(body, place, operands, outs, flops=0, scratch=(), fixed=True, home=False, alias=None):
    if fixed:
        operands = [pltpu.with_memory_space_constraint(a, pltpu.VMEM) for a in operands]
    single = not isinstance(outs, list)
    outs = [outs] if single else outs
    moved = sum(math.prod(a.shape) * 2 for a in (*operands, *outs))
    got = pl.pallas_call(
        body,
        out_shape=outs if home else [pltpu.VMEM(o.shape, o.dtype) for o in outs],
        in_specs=[SMEM] + [VMEM] * len(operands),
        out_specs=[VMEM] * len(outs),
        scratch_shapes=list(scratch),
        input_output_aliases=alias or {},
        cost_estimate=pl.CostEstimate(flops=flops, bytes_accessed=moved, transcendentals=0),
        compiler_params=pltpu.CompilerParams(vmem_limit_bytes=VMEM_LIMIT),
    )(place, *operands)
    return got[0] if single else got


def first_blocks(own):
    return own, shift(own, "x", 1), shift(own, "x", -1), shift(own, "yl", 1)


def more_blocks(first):
    _, _, r30, r01 = first
    return shift(r30, "x", -1), shift(r01, "x", 1), shift(r30, "yl", 1)


def last_block(more):
    _, r11, r31 = more
    half = (r11.shape[0] // 2 + 15) // 16 * 16
    return shift(r11[:half], "x", 1), shift(r31[half:], "x", -1)


def packing(rows, cols):
    width = cols // LANES * LANES
    rest = cols - width
    groups = width // rest
    return width, rest, groups, rows // groups


def pack(block, out):
    rows, cols = block.shape
    width, rest, groups, height = packing(rows, cols)
    out[:rows] = block[:, :width].astype(BF16)
    for g in range(groups):
        out[rows:, g * rest : (g + 1) * rest] = block[g * height : (g + 1) * height, width:].astype(BF16)


def fill(panel, refs):
    half, cols = panel.shape[1:]
    rows = half // 2
    width, rest, groups, height = packing(rows, cols)
    total = rows + height
    at = 0
    for ref in refs:
        size = ref.shape[0]
        block, begin = divmod(at, total)
        i, base = divmod(block * rows, half)
        main = min(size, rows - begin)
        panel[i, base + begin : base + begin + main, :width] = ref[:main]
        if begin + size == total:
            for g in range(groups):
                low = base + g * height
                panel[i, low : low + height, width:] = ref[main:, g * rest : (g + 1) * rest]
        at += size


def pack_body(place, own, packed, copy):
    value = own[...]
    copy[...] = value
    pack(value.astype(F32), packed)


def chunk(z, far, size):
    return pl.ds(pl.multiple_of(lax.rem(z + far, RING) * size, 8), size)


def gram_body(place, own, *refs):
    *blocks, keep, send, panel, rows = refs
    fill(panel, blocks)
    z, c = place[0], place[1]
    dims = (((1,), (1,)), ((), ()))

    @pl.loop(0, 2)
    def _(i):
        rows[i] = lax.dot_general(own[...], panel[i], dims, preferred_element_type=F32)

    size = keep.shape[1]
    for side, out in ((c, keep), (1 - c, send)):
        for far in range(RING):
            out[far] = rows[side, chunk(z, far, size), :].astype(BF16)


def gram_partial(place, own, blocks):
    rows, cols = own.shape
    part = array((RING, rows // RING, 2 * rows))
    panel = array((2, 2 * rows, cols))
    scratch = [pltpu.VMEM((2, rows, 2 * rows), F32)]
    return call(gram_body, place, (own, *blocks), [part, part, panel], 8 * rows * rows * cols, scratch)


def pair_body(place, low, low_other, high, high_other, *outs):
    size = low.shape[1]
    for d in range(RING):
        lower = (low[d].astype(F32) + low_other[d].astype(F32)).astype(BF16)
        upper = (high[d].astype(F32) + high_other[d].astype(F32)).astype(BF16)
        if d == FAR:
            outs[d][...] = lower
            outs[d + 1][...] = upper
        else:
            out = outs[d if d < FAR else d + 1]
            out[:size] = lower
            out[size:] = upper


def add(a, b):
    return (a.astype(F32) + b.astype(F32)).astype(BF16)


def ring_sum(part, up, down):
    size = up.shape[0]
    for step in range(FAR - 1, -1, -1):
        up, down = shift(up, "z", -1), shift(down, "z", 1)
        if step == 0:
            total = part[0].astype(F32) + up.astype(F32) + down.astype(F32)
        elif step == FAR - 1:
            one, two = part[step], part[RING - step]
            up = jnp.concatenate([add(one[:size], up), one[size:]], 0)
            down = jnp.concatenate([two[:size], add(two[size:], down)], 0)
        else:
            up, down = add(part[step], up), add(part[RING - step], down)
    return total.astype(BF16)


def group_body(place, *refs):
    *pieces, out = refs
    for i, ref in enumerate(pieces):
        out[i] = ref[...]


def rows_body(place, low, high, group, other, near, far, total):
    z, c = place[0], place[1]
    size = near.shape[1] // RING
    for side, ref in ((c, group), (1 - c, other)):
        for i in range(RING - 1):
            where = chunk(z, i if i < FAR else i + 1, size)
            near[side, where, :] = ref[i, :size]
            far[side, where, :] = ref[i, size:]
    for side in range(2):
        near[side, chunk(z, FAR, size), :] = jnp.zeros((size, near.shape[2]), BF16)
        far[side, chunk(z, FAR, size), :] = jnp.zeros((size, near.shape[2]), BF16)
    total[...] = jnp.zeros(total.shape, F32)

    @pl.loop(0, 2)
    def _(i):
        total[...] += jnp.dot(near[i], low[i], preferred_element_type=F32) + jnp.dot(
            far[i], high[i], preferred_element_type=F32
        )


def update_body(place, own, low, high, near, far, before, *refs):
    ends, (near_out, far_out, w_high, w_low, total) = refs[:4], refs[4:]
    z, c = place[0], place[1]
    size = near.shape[1] // RING
    where = chunk(z, FAR, size)
    for side, lower, upper in ((c, ends[0], ends[1]), (1 - c, ends[2], ends[3])):
        near_out[side, where, :] = lower[...]
        far_out[side, where, :] = upper[...]
    acc = jnp.zeros((size, own.shape[1]), F32)
    for gram, panel in ((near_out, low), (far_out, high)):
        for i in range(2):
            acc += jnp.dot(gram[i, where, :], panel[i], preferred_element_type=F32)
    total[...] = before[...]
    total[where, :] = acc
    w = coef_b * own[...].astype(F32) + coef_c * total[...]
    pack(w, w_high)
    w_low[...] = (w - w.astype(BF16).astype(F32)).astype(BF16)


def near_body(place, own, w_low, gram, *refs):
    *blocks, total, panel = refs
    rows = own.shape[0]
    fill(panel, blocks)
    acc = coef_a * own[...].astype(F32)
    acc += jnp.dot(gram[0][:, :rows], w_low[...], preferred_element_type=F32)
    total[...] = acc

    @pl.loop(0, 2)
    def _(i):
        total[...] += jnp.dot(gram[i], panel[i], preferred_element_type=F32)


def side_body(place, before, gram, *refs):
    *blocks, total, panel = refs
    fill(panel, blocks)
    total[...] = before[...] + jnp.dot(gram[0], panel[0], preferred_element_type=F32)


def far_body(place, before, gram, *refs):
    *blocks, out, panel = refs
    fill(panel, blocks)
    acc = before[...] + jnp.dot(gram[1], panel[0], preferred_element_type=F32)
    rows, cols = out.shape
    factor = 0.2 * math.sqrt(max(rows * PANEL, cols * math.prod(SIZES[n] for n in COL)))
    out[...] = (acc * factor).astype(BF16)


def newton_step(matrix):
    rows, cols = matrix.shape
    size = rows // RING
    place = jnp.stack([lax.axis_index("z"), lax.axis_index("c")]).astype(jnp.int32)
    width, _, _, height = packing(rows, cols)
    flat = array((rows + height, width))
    block = array((rows, cols))

    packed, own = call(pack_body, place, (matrix,), [flat, block], fixed=False)
    first = lax.optimization_barrier(first_blocks(packed))
    keep, send, low = gram_partial(place, own, first)
    halves = [keep, shift(send, "c", 1)]
    more = lax.optimization_barrier(more_blocks(first))
    last = last_block(more)
    keep, send, high = gram_partial(place, own, (*more, *last))
    halves += [keep, shift(send, "c", 1)]

    one, two = array((size, 2 * rows)), array((2 * size, 2 * rows))
    parts = call(pair_body, place, halves, [two] * FAR + [one] * 2 + [two] * (FAR - 1))
    part = {d: parts[d if d < FAR else d + 1] for d in range(RING) if d != FAR}
    mine = ring_sum(part, parts[FAR], parts[FAR + 1])
    mine = add(mine, shift(mine, "yh", 1))

    ring = {0: mine}
    up, down = mine, mine
    for step in range(1, FAR):
        up, down = lax.optimization_barrier((shift(up, "z", 1), shift(down, "z", -1)))
        ring[step], ring[RING - step] = up, down
    ends = [shift(up[:size], "z", 1)]
    ends.append(shift(down[size:], "z", -1))
    pieces = [ring[d] for d in range(RING) if d != FAR]
    group = call(group_body, place, pieces, array((RING - 1, 2 * size, 2 * rows)))
    ends += [shift(p, "c", 1) for p in ends]

    sums = array((rows, cols), F32)
    wide = array((2, rows, 2 * rows))
    work = 4 * rows * rows * cols
    other = shift(group, "c", 1)
    gram_near, gram_far, total = call(rows_body, place, (low, high, group, other), [wide, wide, sums], 4 * work)
    gram_near, gram_far, w_high, w_low = call(
        update_body,
        place,
        (own, low, high, gram_near, gram_far, total, *ends),
        [wide, wide, flat, block],
        work // 2,
        [pltpu.VMEM((rows, cols), F32)],
        alias={4: 0, 5: 1},
    )

    def panel(count):
        return [pltpu.VMEM((count, 2 * rows, cols), BF16)]

    near = lax.optimization_barrier(first_blocks(w_high))
    total = call(near_body, place, (own, w_low, gram_near, *near), sums, 5 * work // 2, panel(2))
    side = lax.optimization_barrier(more_blocks(near))
    total = call(side_body, place, (total, gram_far, *side[:2]), sums, work, panel(1))
    ends = last_block(side)
    return call(far_body, place, (total, gram_far, side[2], *ends), block, work, panel(1), home=True)


def solution(mesh):
    fine = Mesh(mesh.devices.reshape(tuple(SIZES.values())), AXES)
    return jax.shard_map(newton_step, mesh=fine, in_specs=(P(ROW, COL),), out_specs=P(ROW, COL), check_vma=False)
```

```python
import itertools
import math

import jax
import jax.numpy as jnp
from jax import lax
from jax.experimental import pallas as pl
from jax.experimental.pallas import tpu as pltpu
from jax.sharding import Mesh
from jax.sharding import PartitionSpec as P


coef_a = 3.4445
coef_b = -4.775
coef_c = 2.0315


SIZES = {"x": 4, "yl": 2, "z": 8, "yh": 2, "c": 2}
AXES = tuple(SIZES)
ROW = ("x", "yl")
COL = ("z", "yh", "c")
RING = SIZES["z"]
PANEL = SIZES["x"] * SIZES["yl"]
FAR = RING // 2
LANES = 128
VMEM_LIMIT = 14 << 20

F32 = jnp.float32
BF16 = jnp.bfloat16
VMEM = pl.BlockSpec(memory_space=pltpu.VMEM)
SMEM = pl.BlockSpec(memory_space=pltpu.SMEM)


def array(shape, kind=BF16):
    return jax.ShapeDtypeStruct(shape, kind)


def shift(value, axis, step):
    size = SIZES[axis]
    return lax.ppermute(value, axis, [((i + step) % size, i) for i in range(size)])


def fetch(value, axes, source):
    sizes = [SIZES[a] for a in axes]

    def flat(position):
        index = 0
        for p, n in zip(position, sizes, strict=True):
            index = index * n + p % n
        return index

    places = list(itertools.product(*(range(n) for n in sizes)))
    return lax.ppermute(value, axes, [(flat(source(*p)), flat(p)) for p in places])


def call(body, place, operands, outs, flops=0, scratch=(), fixed=True, home=False, alias=None):
    if fixed:
        operands = [pltpu.with_memory_space_constraint(a, pltpu.VMEM) for a in operands]
    single = not isinstance(outs, list)
    outs = [outs] if single else outs
    moved = sum(math.prod(a.shape) * 2 for a in (*operands, *outs))
    got = pl.pallas_call(
        body,
        out_shape=outs if home else [pltpu.VMEM(o.shape, o.dtype) for o in outs],
        in_specs=[SMEM] + [VMEM] * len(operands),
        out_specs=[VMEM] * len(outs),
        scratch_shapes=list(scratch),
        input_output_aliases=alias or {},
        cost_estimate=pl.CostEstimate(flops=flops, bytes_accessed=moved, transcendentals=0),
        compiler_params=pltpu.CompilerParams(vmem_limit_bytes=VMEM_LIMIT),
    )(place, *operands)
    return got[0] if single else got


def first_blocks(own):
    return own, shift(own, "x", 1), shift(own, "x", -1), shift(own, "yl", 1)


def more_blocks(first):
    _, _, r30, r01 = first
    r20 = shift(r30, "x", -1)
    r11 = shift(r01, "x", 1)
    r31 = shift(r30, "yl", 1)
    return r20, r11, r31


def last_block(more):
    _, r11, r31 = more
    half = (r11.shape[0] // 2 + 15) // 16 * 16
    return shift(r11[:half], "x", 1), shift(r31[half:], "x", -1)


def packing(rows, cols):
    width = cols // LANES * LANES
    rest = cols - width
    groups = width // rest
    return width, rest, groups, rows // groups


def pack(block, out):
    rows, cols = block.shape
    width, rest, groups, height = packing(rows, cols)
    out[:rows] = block[:, :width].astype(BF16)
    for g in range(groups):
        out[rows:, g * rest : (g + 1) * rest] = block[g * height : (g + 1) * height, width:].astype(BF16)


def fill(panel, refs):
    half, cols = panel.shape[1:]
    rows = half // 2
    width, rest, groups, height = packing(rows, cols)
    total = rows + height
    at = 0
    for ref in refs:
        size = ref.shape[0]
        block, begin = divmod(at, total)
        i, base = divmod(block * rows, half)
        main = min(size, rows - begin)
        panel[i, base + begin : base + begin + main, :width] = ref[:main]
        if begin + size == total:
            for g in range(groups):
                low = base + g * height
                panel[i, low : low + height, width:] = ref[main:, g * rest : (g + 1) * rest]
        at += size


def pack_body(place, own, packed, copy):
    value = own[...]
    copy[...] = value
    pack(value.astype(F32), packed)


def chunk(z, far, size):
    return pl.ds(pl.multiple_of(lax.rem(z + far, RING) * size, 8), size)


DIMS = (((1,), (1,)), ((), ()))


def gram_body(place, own, *refs):
    *blocks, keep, send, panel, partner, beside, rows, mixed = refs
    fill(panel, blocks)
    z, c = place[0], place[1]
    height = own.shape[0]
    mixed[:height] = panel[0, height:]
    mixed[height:] = panel[1, :height]

    @pl.loop(0, 2)
    def _(i):
        rows[i] = lax.dot_general(own[...], panel[i], DIMS, preferred_element_type=F32)

    partner[...] = lax.dot_general(panel[1, height:], mixed[...], DIMS, preferred_element_type=F32)
    beside[...] = lax.dot_general(panel[0, height:], panel[1, :height], DIMS, preferred_element_type=F32)
    split_units(z, c, rows, keep, send)


def split_units(z, c, rows, keep, send):
    size = keep.shape[1]
    for side, out in ((c, keep), (1 - c, send)):
        for far in range(RING):
            out[far] = rows[side, chunk(z, far, size), :].astype(BF16)


def late_body(place, own, partner, beside, block, keep, send, rows, panel):
    z, c = place[0], place[1]
    height = own.shape[0]
    fill(panel, [block])
    rows[0] = partner[...]
    rows[1, :, :height] = lax.dot_general(own[...], panel[0, :height], DIMS, preferred_element_type=F32)
    rows[1, :, height:] = beside[...]
    split_units(z, c, rows, keep, send)


def panel_body(place, *refs):
    *blocks, panel = refs
    fill(panel, blocks)


def pair_body(place, low, low_other, high, high_other, *outs):
    size = low.shape[1]
    for d in range(RING):
        lower = (low[d].astype(F32) + low_other[d].astype(F32)).astype(BF16)
        upper = (high[d].astype(F32) + high_other[d].astype(F32)).astype(BF16)
        if d == FAR:
            outs[d][...] = lower
            outs[d + 1][...] = upper
        else:
            out = outs[d if d < FAR else d + 1]
            out[:size] = lower
            out[size:] = upper


def add(a, b):
    return (a.astype(F32) + b.astype(F32)).astype(BF16)


def ring_sum(part, up, down):
    size = up.shape[0]
    for step in range(FAR - 1, -1, -1):
        up = shift(up, "z", -1)
        down = shift(down, "z", 1)
        if step == 0:
            total = part[0].astype(F32) + up.astype(F32) + down.astype(F32)
        elif step == FAR - 1:
            one, two = part[step], part[RING - step]
            up = jnp.concatenate([add(one[:size], up), one[size:]], 0)
            down = jnp.concatenate([two[:size], add(two[size:], down)], 0)
        else:
            up, down = add(part[step], up), add(part[RING - step], down)
    return total.astype(BF16)


def group_body(place, *refs):
    *pieces, out = refs
    for i, ref in enumerate(pieces):
        out[i] = ref[...]


def rows_body(place, low, high, group, other, near, far, total):
    z, c = place[0], place[1]
    size = near.shape[1] // RING
    for side, ref in ((c, group), (1 - c, other)):
        for i in range(RING - 1):
            where = chunk(z, i if i < FAR else i + 1, size)
            near[side, where, :] = ref[i, :size]
            far[side, where, :] = ref[i, size:]
    for side in range(2):
        near[side, chunk(z, FAR, size), :] = jnp.zeros((size, near.shape[2]), BF16)
        far[side, chunk(z, FAR, size), :] = jnp.zeros((size, near.shape[2]), BF16)
    total[...] = jnp.zeros(total.shape, F32)

    @pl.loop(0, 2)
    def _(i):
        total[...] += jnp.dot(near[i], low[i], preferred_element_type=F32) + jnp.dot(
            far[i], high[i], preferred_element_type=F32
        )


def update_body(place, own, low, high, near, far, before, *refs):
    mine, other, near_out, far_out, w_high, w_low, total = refs
    z, c = place[0], place[1]
    size = near.shape[1] // RING
    where = chunk(z, FAR, size)
    for side, ref in ((c, mine), (1 - c, other)):
        near_out[side, where, :] = ref[:size]
        far_out[side, where, :] = ref[size:]
    acc = jnp.zeros((size, own.shape[1]), F32)
    for gram, panel in ((near_out, low), (far_out, high)):
        for i in range(2):
            acc += jnp.dot(gram[i, where, :], panel[i], preferred_element_type=F32)
    total[...] = before[...]
    total[where, :] = acc
    w = coef_b * own[...].astype(F32) + coef_c * total[...]
    pack(w, w_high)
    w_low[...] = (w - w.astype(BF16).astype(F32)).astype(BF16)


def near_body(place, own, w_low, gram, *refs):
    *blocks, total, panel = refs
    rows = own.shape[0]
    fill(panel, blocks)
    acc = coef_a * own[...].astype(F32)
    acc += jnp.dot(gram[0][:, :rows], w_low[...], preferred_element_type=F32)
    total[...] = acc

    @pl.loop(0, 2)
    def _(i):
        total[...] += jnp.dot(gram[i], panel[i], preferred_element_type=F32)


def side_body(place, before, gram, *refs):
    *blocks, total, panel = refs
    fill(panel, blocks)
    total[...] = before[...] + jnp.dot(gram[0], panel[0], preferred_element_type=F32)


def far_body(place, before, gram, *refs):
    *blocks, out, panel = refs
    fill(panel, blocks)
    acc = before[...] + jnp.dot(gram[1], panel[0], preferred_element_type=F32)
    rows, cols = out.shape
    factor = 0.2 * math.sqrt(max(rows * PANEL, cols * math.prod(SIZES[n] for n in COL)))
    out[...] = (acc * factor).astype(BF16)


def newton_step(matrix):
    rows, cols = matrix.shape
    size = rows // RING
    place = jnp.stack([lax.axis_index("z"), lax.axis_index("c")]).astype(jnp.int32)
    width, _, _, height = packing(rows, cols)
    flat = array((rows + height, width))
    block = array((rows, cols))

    packed, own = call(pack_body, place, (matrix,), [flat, block], fixed=False)
    first = lax.optimization_barrier(first_blocks(packed))
    r21 = fetch(packed, ("x", "yl"), lambda x, y: (x + 2, y + 1))
    part = array((RING, size, 2 * rows))
    wide = array((2, rows, 2 * rows))
    panel = array((2, 2 * rows, cols))
    work = 4 * rows * rows * cols
    keep, send, low, partner, beside = call(
        gram_body,
        place,
        (own, *first),
        [part, part, panel, array((rows, 2 * rows), F32), array((rows, rows), F32)],
        7 * work // 2,
        [pltpu.VMEM(wide.shape, F32), pltpu.VMEM((2 * rows, cols), BF16)],
    )
    halves = [keep, shift(send, "c", 1)]
    keep, send = call(
        late_body,
        place,
        (own, partner, beside, r21),
        [part, part],
        work // 2,
        [pltpu.VMEM(wide.shape, F32), pltpu.VMEM((1, 2 * rows, cols), BF16)],
    )
    halves += [keep, shift(send, "c", 1)]
    r20, r11, r31 = more_blocks(first)
    high = call(panel_body, place, (r11, r31, r21, r20), panel)
    one, two = array((size, 2 * rows)), array((2 * size, 2 * rows))
    parts = call(pair_body, place, halves, [two] * FAR + [one] * 2 + [two] * (FAR - 1))
    part = {d: parts[d if d < FAR else d + 1] for d in range(RING) if d != FAR}
    mine = ring_sum(part, parts[FAR], parts[FAR + 1])
    ahead = mine[size:]
    same = fetch(ahead, ("x", "yl", "c"), lambda x, y, c: (x, y + 1, c) if c == 0 else (x - 1, y, c))
    cross = fetch(
        ahead, ("x", "yl", "yh", "c"), lambda x, y, h, c: (x, y + 1, h + 1, c) if c == 0 else (x - 1, y, h + 1, c)
    )
    mine = add(mine, shift(mine, "yh", 1))
    ahead = add(same, cross)
    left = lax.broadcasted_iota(jnp.int32, ahead.shape, 1) < rows
    ahead = jnp.where((place[1] == 1) & left, mine[size:], ahead)
    mine = jnp.concatenate([mine[:size], ahead], 0)

    ring = {0: mine}
    up, down = mine, mine
    for step in range(1, FAR):
        up = shift(up, "z", 1)
        down = shift(down, "z", -1)
        ring[step], ring[RING - step] = up, down
    ends = [shift(up[:size], "z", 1)]
    ends.append(shift(down[size:], "z", -1))
    pieces = [ring[d] for d in range(RING) if d != FAR]
    group = call(group_body, place, pieces, array((RING - 1, 2 * size, 2 * rows)))
    ends = jnp.concatenate(ends, 0)

    sums = array((rows, cols), F32)
    other = shift(group, "c", 1)
    gram_near, gram_far, total = call(rows_body, place, (low, high, group, other), [wide, wide, sums], 4 * work)
    gram_near, gram_far, w_high, w_low = call(
        update_body,
        place,
        (own, low, high, gram_near, gram_far, total, ends, shift(ends, "c", 1)),
        [wide, wide, flat, block],
        work // 2,
        [pltpu.VMEM((rows, cols), F32)],
        alias={4: 0, 5: 1},
    )

    def room(count):
        return [pltpu.VMEM((count, 2 * rows, cols), BF16)]

    near = lax.optimization_barrier(first_blocks(w_high))
    total = call(near_body, place, (own, w_low, gram_near, *near), sums, 5 * work // 2, room(2))
    side = lax.optimization_barrier(more_blocks(near))
    total = call(side_body, place, (total, gram_far, *side[1:]), sums, work, room(1))
    ends = last_block(side)
    return call(far_body, place, (total, gram_far, *ends, side[0]), block, work, room(1), home=True)


def solution(mesh):
    fine = Mesh(mesh.devices.reshape(tuple(SIZES.values())), AXES)
    return jax.shard_map(newton_step, mesh=fine, in_specs=(P(ROW, COL),), out_specs=P(ROW, COL), check_vma=False)
```

```python
import itertools
import math

import jax
import jax.numpy as jnp
from jax import lax
from jax.experimental import pallas as pl
from jax.experimental.pallas import tpu as pltpu
from jax.sharding import Mesh
from jax.sharding import PartitionSpec as P


coef_a = 3.4445
coef_b = -4.775
coef_c = 2.0315


SIZES = {"x": 4, "yl": 2, "z": 8, "yh": 2, "c": 2}
AXES = tuple(SIZES)
ROW = ("x", "yl")
COL = ("z", "yh", "c")
RING = SIZES["z"]
PANEL = SIZES["x"] * SIZES["yl"]
FAR = RING // 2
LANES = 128
VMEM_LIMIT = 14 << 20

F32 = jnp.float32
BF16 = jnp.bfloat16
VMEM = pl.BlockSpec(memory_space=pltpu.VMEM)
SMEM = pl.BlockSpec(memory_space=pltpu.SMEM)


def array(shape, kind=BF16):
    return jax.ShapeDtypeStruct(shape, kind)


def shift(value, axis, step):
    size = SIZES[axis]
    return lax.ppermute(value, axis, [((i + step) % size, i) for i in range(size)])


def fetch(value, axes, source):
    sizes = [SIZES[a] for a in axes]

    def flat(position):
        index = 0
        for p, n in zip(position, sizes, strict=True):
            index = index * n + p % n
        return index

    places = list(itertools.product(*(range(n) for n in sizes)))
    return lax.ppermute(value, axes, [(flat(source(*p)), flat(p)) for p in places])


def call(body, place, operands, outs, flops=0, scratch=(), fixed=True, home=False, alias=None):
    if fixed:
        operands = [pltpu.with_memory_space_constraint(a, pltpu.VMEM) for a in operands]
    single = not isinstance(outs, list)
    outs = [outs] if single else outs
    moved = sum(math.prod(a.shape) * 2 for a in (*operands, *outs))
    got = pl.pallas_call(
        body,
        out_shape=outs if home else [pltpu.VMEM(o.shape, o.dtype) for o in outs],
        in_specs=[SMEM] + [VMEM] * len(operands),
        out_specs=[VMEM] * len(outs),
        scratch_shapes=list(scratch),
        input_output_aliases=alias or {},
        cost_estimate=pl.CostEstimate(flops=flops, bytes_accessed=moved, transcendentals=0),
        compiler_params=pltpu.CompilerParams(vmem_limit_bytes=VMEM_LIMIT),
    )(place, *operands)
    return got[0] if single else got


def first_blocks(own):
    near = shift(own, "x", 1), shift(own, "x", -1), shift(own, "yl", 1)
    return lax.optimization_barrier(near), shift(own, "x", 2)


def more_blocks(near, r20):
    _, _, r01 = near
    r11 = shift(r01, "x", 1)
    r31 = shift(r01, "x", -1)
    r21 = shift(r20, "yl", 1)
    return r11, r31, r21


def packing(rows, cols):
    width = cols // LANES * LANES
    rest = cols - width
    groups = width // rest
    return width, rest, groups, rows // groups


def pack(block, out):
    rows, cols = block.shape
    width, rest, groups, height = packing(rows, cols)
    out[:rows] = block[:, :width].astype(BF16)
    for g in range(groups):
        out[rows:, g * rest : (g + 1) * rest] = block[g * height : (g + 1) * height, width:].astype(BF16)


def fill(panel, refs):
    half, cols = panel.shape[1:]
    rows = half // 2
    width, rest, groups, height = packing(rows, cols)
    total = rows + height
    at = 0
    for ref in refs:
        size = ref.shape[0]
        block, begin = divmod(at, total)
        i, base = divmod(block * rows, half)
        main = min(size, rows - begin)
        panel[i, base + begin : base + begin + main, :width] = ref[:main]
        if begin + size == total:
            for g in range(groups):
                low = base + g * height
                panel[i, low : low + height, width:] = ref[main:, g * rest : (g + 1) * rest]
        at += size


def pack_body(place, own, packed, copy):
    value = own[...]
    copy[...] = value
    pack(value.astype(F32), packed)


def chunk(z, far, size):
    return pl.ds(pl.multiple_of(lax.rem(z + far, RING) * size, 8), size)


DIMS = (((1,), (1,)), ((), ()))


def gram_body(place, own, *refs):
    *blocks, keep, send, panel, partner, rows, mixed = refs
    fill(panel, blocks)
    z, c = place[0], place[1]
    height = own.shape[0]
    mixed[:height] = panel[0, height:]
    mixed[height:] = panel[1, :height]

    @pl.loop(0, 2)
    def _(i):
        rows[i] = lax.dot_general(own[...], panel[i], DIMS, preferred_element_type=F32)

    partner[...] = lax.dot_general(panel[1, height:], mixed[...], DIMS, preferred_element_type=F32)
    split_units(z, c, rows, keep, send)


def split_units(z, c, rows, keep, send):
    size = keep.shape[1]
    for side, out in ((c, keep), (1 - c, send)):
        for far in range(RING):
            out[far] = rows[side, chunk(z, far, size), :].astype(BF16)


def late_body(place, own, low, partner, block, keep, send, rows, panel):
    z, c = place[0], place[1]
    height = own.shape[0]
    fill(panel, [block])
    rows[0] = partner[...]
    rows[1, :, :height] = lax.dot_general(low[1, height:], panel[0, :height], DIMS, preferred_element_type=F32)
    rows[1, :, height:] = lax.dot_general(own[...], panel[0, :height], DIMS, preferred_element_type=F32)
    split_units(z, c, rows, keep, send)


def panel_body(place, low, *refs):
    *blocks, panel, high = refs
    fill(high, blocks)
    for i in range(2):
        panel[i] = low[i]
        panel[i + 2] = high[i]


def pair_body(place, low, low_other, high, high_other, *outs):
    size = low.shape[1]
    for d in range(RING):
        lower = (low[d].astype(F32) + low_other[d].astype(F32)).astype(BF16)
        upper = (high[d].astype(F32) + high_other[d].astype(F32)).astype(BF16)
        if d == FAR:
            outs[d][...] = lower
            outs[d + 1][...] = upper
        else:
            out = outs[d if d < FAR else d + 1]
            out[:size] = lower
            out[size:] = upper


def add(a, b):
    return (a.astype(F32) + b.astype(F32)).astype(BF16)


def ring_sum(part, up, down):
    size = up.shape[0]
    for step in range(FAR - 1, -1, -1):
        up = shift(up, "z", -1)
        down = shift(down, "z", 1)
        if step == 0:
            total = part[0].astype(F32) + up.astype(F32) + down.astype(F32)
        elif step == FAR - 1:
            one, two = part[step], part[RING - step]
            up = jnp.concatenate([add(one[:size], up), one[size:]], 0)
            down = jnp.concatenate([two[:size], add(two[size:], down)], 0)
        else:
            up, down = add(part[step], up), add(part[RING - step], down)
    return total.astype(BF16)


def group_body(place, *refs):
    *pieces, out = refs
    for i, ref in enumerate(pieces):
        out[i] = ref[...]


def lay(gram, side, group, z):
    size = gram.shape[1] // RING
    for i in range(RING - 1):
        where = chunk(z, i if i < FAR else i + 1, size)
        gram[side, where, :] = group[i, :size]
        gram[side + 2, where, :] = group[i, size:]
    for half in (side, side + 2):
        gram[half, chunk(z, FAR, size), :] = jnp.zeros((size, gram.shape[2]), BF16)


def own_rows_body(place, panel, group, gram, total):
    z, c = place[0], place[1]
    lay(gram, c, group, z)
    total[...] = jnp.zeros(total.shape, F32)

    @pl.loop(0, 2)
    def _(i):
        total[...] += jnp.dot(gram[c + 2 * i], panel[c + 2 * i], preferred_element_type=F32)


def other_rows_body(place, panel, group, before_gram, before, gram, total):
    z, side = place[0], 1 - place[1]
    lay(gram, side, group, z)

    @pl.loop(0, 2)
    def _(i):
        total[...] += jnp.dot(gram[side + 2 * i], panel[side + 2 * i], preferred_element_type=F32)


def update_body(place, own, panel, before_gram, before, mine, other, gram, w_high, w_low, total, acc):
    z, c = place[0], place[1]
    size = gram.shape[1] // RING
    where = chunk(z, FAR, size)
    for side, ref in ((c, mine), (1 - c, other)):
        gram[side, where, :] = ref[:size]
        gram[side + 2, where, :] = ref[size:]
    acc[...] = jnp.zeros(acc.shape, F32)

    @pl.loop(0, 4)
    def _(i):
        acc[...] += jnp.dot(gram[i, where, :], panel[i], preferred_element_type=F32)

    total[...] = before[...]
    total[where, :] = acc[...]
    w = coef_b * own[...].astype(F32) + coef_c * total[...]
    pack(w, w_high)
    w_low[...] = (w - w.astype(BF16).astype(F32)).astype(BF16)


def near_body(place, own, w_low, gram, *refs):
    *blocks, total, panel = refs
    rows = own.shape[0]
    fill(panel, blocks)
    acc = coef_a * own[...].astype(F32)
    total[...] = acc + jnp.dot(gram[0][:, :rows], w_low[...], preferred_element_type=F32)

    @pl.loop(0, 2)
    def _(i):
        total[...] += jnp.dot(gram[i], panel[i], preferred_element_type=F32)


def side_body(place, before, gram, block, total, panel):
    rows = total.shape[0]
    fill(panel, [block])
    total[...] = before[...] + jnp.dot(gram[3][:, rows:], panel[0, :rows], preferred_element_type=F32)


def far_body(place, before, gram, r11, r31, r21, out, panel):
    rows, cols = out.shape
    fill(panel, (r11, r31, r21))
    acc = before[...] + jnp.dot(gram[2], panel[0], preferred_element_type=F32)
    acc += jnp.dot(gram[3][:, :rows], panel[1, :rows], preferred_element_type=F32)
    factor = 0.2 * math.sqrt(max(rows * PANEL, cols * math.prod(SIZES[n] for n in COL)))
    out[...] = (acc * factor).astype(BF16)


def newton_step(matrix):
    rows, cols = matrix.shape
    size = rows // RING
    place = jnp.stack([lax.axis_index("z"), lax.axis_index("c")]).astype(jnp.int32)
    width, _, _, height = packing(rows, cols)
    flat = array((rows + height, width))
    block = array((rows, cols))

    packed, own = call(pack_body, place, (matrix,), [flat, block], fixed=False)
    near, r20 = first_blocks(packed)
    part = array((RING, size, 2 * rows))
    wide = array((4, rows, 2 * rows))
    sums = array((rows, cols), F32)
    work = 4 * rows * rows * cols

    def room(count, kind=BF16, width=cols):
        return pltpu.VMEM((count, 2 * rows, width), kind)

    pairs = pltpu.VMEM((2, rows, 2 * rows), F32)
    keep, send, low, partner = call(
        gram_body,
        place,
        (own, packed, *near),
        [part, part, array((2, 2 * rows, cols)), array((rows, 2 * rows), F32)],
        3 * work,
        [pairs, pltpu.VMEM((2 * rows, cols), BF16)],
    )
    halves = [keep, shift(send, "c", 1)]
    keep, send = call(late_body, place, (own, low, partner, r20), [part, part], work, [pairs, room(1)])
    halves += [keep, shift(send, "c", 1)]
    r11, r31, r21 = more_blocks(near, r20)
    panel = call(panel_body, place, (low, r11, r31, r21, r20), array((4, 2 * rows, cols)), 0, [room(2)])
    one, two = array((size, 2 * rows)), array((2 * size, 2 * rows))
    parts = call(pair_body, place, halves, [two] * FAR + [one] * 2 + [two] * (FAR - 1))
    part = {d: parts[d if d < FAR else d + 1] for d in range(RING) if d != FAR}
    mine = ring_sum(part, parts[FAR], parts[FAR + 1])
    ahead = mine[size:]
    same = shift(ahead, "yl", 1)
    cross = fetch(ahead, ("yl", "yh"), lambda y, h: (y + 1, h + 1))
    mine = add(mine, shift(mine, "yh", 1))
    ahead = add(same, cross)
    right = lax.broadcasted_iota(jnp.int32, ahead.shape, 1) >= rows
    ahead = jnp.where((place[1] == 1) & right, mine[size:], ahead)
    mine = jnp.concatenate([mine[:size], ahead], 0)

    ring = {0: mine}
    up, down = mine, mine
    for step in range(1, FAR):
        up = shift(up, "z", 1)
        down = shift(down, "z", -1)
        ring[step], ring[RING - step] = up, down
    ends = [shift(up[:size], "z", 1)]
    ends.append(shift(down[size:], "z", -1))
    pieces = [ring[d] for d in range(RING) if d != FAR]
    group = call(group_body, place, pieces, array((RING - 1, 2 * size, 2 * rows)))
    ends = jnp.concatenate(ends, 0)

    other = shift(group, "c", 1)
    gram, total = call(own_rows_body, place, (panel, group), [wide, sums], 2 * work)
    gram, total = call(other_rows_body, place, (panel, other, gram, total), [wide, sums], 2 * work, alias={3: 0, 4: 1})
    gram, w_high, w_low = call(
        update_body,
        place,
        (own, panel, gram, total, ends, shift(ends, "c", 1)),
        [wide, flat, block],
        work // 2,
        [pltpu.VMEM((rows, cols), F32), pltpu.VMEM((size, cols), F32)],
        alias={3: 0},
    )

    near, r20 = first_blocks(w_high)
    total = call(near_body, place, (own, w_low, gram, w_high, *near), sums, 5 * work // 2, [room(2)])
    ends = more_blocks(near, r20)
    total = call(side_body, place, (total, gram, r20), sums, work // 2, [room(1)])
    return call(far_body, place, (total, gram, *ends), block, 3 * work // 2, [room(2)], home=True)


def solution(mesh):
    fine = Mesh(mesh.devices.reshape(tuple(SIZES.values())), AXES)
    return jax.shard_map(newton_step, mesh=fine, in_specs=(P(ROW, COL),), out_specs=P(ROW, COL), check_vma=False)
```

```python
import itertools
import math

import jax
import jax.numpy as jnp
from jax import lax
from jax.experimental import pallas as pl
from jax.experimental.pallas import tpu as pltpu
from jax.sharding import Mesh
from jax.sharding import PartitionSpec as P


coef_a = 3.4445
coef_b = -4.775
coef_c = 2.0315


SIZES = {"x": 4, "yl": 2, "z": 8, "yh": 2, "c": 2}
AXES = tuple(SIZES)
ROW = ("x", "yl")
COL = ("z", "yh", "c")
RING = SIZES["z"]
PANEL = SIZES["x"] * SIZES["yl"]
FAR = RING // 2
LANES = 128
VMEM_LIMIT = 14 << 20

F32 = jnp.float32
BF16 = jnp.bfloat16
VMEM = pl.BlockSpec(memory_space=pltpu.VMEM)
SMEM = pl.BlockSpec(memory_space=pltpu.SMEM)


def array(shape, kind=BF16):
    return jax.ShapeDtypeStruct(shape, kind)


def shift(value, axis, step):
    size = SIZES[axis]
    return lax.ppermute(value, axis, [((i + step) % size, i) for i in range(size)])


def fetch(value, axes, source):
    sizes = [SIZES[a] for a in axes]

    def flat(position):
        index = 0
        for p, n in zip(position, sizes, strict=True):
            index = index * n + p % n
        return index

    places = list(itertools.product(*(range(n) for n in sizes)))
    return lax.ppermute(value, axes, [(flat(source(*p)), flat(p)) for p in places])


def call(body, place, operands, outs, flops=0, scratch=(), fixed=True, home=False, alias=None):
    if fixed:
        operands = [pltpu.with_memory_space_constraint(a, pltpu.VMEM) for a in operands]
    single = not isinstance(outs, list)
    outs = [outs] if single else outs
    moved = sum(math.prod(a.shape) * 2 for a in (*operands, *outs))
    got = pl.pallas_call(
        body,
        out_shape=outs if home else [pltpu.VMEM(o.shape, o.dtype) for o in outs],
        in_specs=[SMEM] + [VMEM] * len(operands),
        out_specs=[VMEM] * len(outs),
        scratch_shapes=list(scratch),
        input_output_aliases=alias or {},
        cost_estimate=pl.CostEstimate(flops=flops, bytes_accessed=moved, transcendentals=0),
        compiler_params=pltpu.CompilerParams(vmem_limit_bytes=VMEM_LIMIT),
    )(place, *operands)
    return got[0] if single else got


def first_blocks(own):
    near = shift(own, "x", 1), shift(own, "x", -1), shift(own, "yl", 1)
    return lax.optimization_barrier(near), shift(own, "x", 2)


def more_blocks(near, r20, spare):
    r10, r30, r01 = near
    r11 = shift(r10, "yl", 1) if spare else shift(r01, "x", 1)
    r31 = shift(r30, "yl", 1) if spare else shift(r01, "x", -1)
    r21 = shift(r20, "yl", 1)
    return r11, r31, r21


def packing(rows, cols):
    width = cols // LANES * LANES
    rest = cols - width
    groups = width // rest
    return width, rest, groups, rows // groups


def pack(block, out):
    rows, cols = block.shape
    width, rest, groups, height = packing(rows, cols)
    out[:rows] = block[:, :width].astype(BF16)
    for g in range(groups):
        out[rows:, g * rest : (g + 1) * rest] = block[g * height : (g + 1) * height, width:].astype(BF16)


def fill(panel, refs):
    half, cols = panel.shape[1:]
    rows = half // 2
    width, rest, groups, height = packing(rows, cols)
    total = rows + height
    at = 0
    for ref in refs:
        size = ref.shape[0]
        block, begin = divmod(at, total)
        i, base = divmod(block * rows, half)
        main = min(size, rows - begin)
        panel[i, base + begin : base + begin + main, :width] = ref[:main]
        if begin + size == total:
            for g in range(groups):
                low = base + g * height
                panel[i, low : low + height, width:] = ref[main:, g * rest : (g + 1) * rest]
        at += size


def pack_body(place, own, packed, copy):
    value = own[...]
    copy[...] = value
    pack(value.astype(F32), packed)


def chunk(z, far, size):
    return pl.ds(pl.multiple_of(lax.rem(z + far, RING) * size, 8), size)


DIMS = (((1,), (1,)), ((), ()))


def gram_body(place, own, *refs):
    *blocks, keep, send, panel, partner, rows, mixed = refs
    fill(panel, blocks)
    z, c = place[0], place[1]
    height = own.shape[0]
    mixed[:height] = panel[0, height:]
    mixed[height:] = panel[1, :height]

    @pl.loop(0, 2)
    def _(i):
        rows[i] = lax.dot_general(own[...], panel[i], DIMS, preferred_element_type=F32)

    partner[...] = lax.dot_general(panel[1, height:], mixed[...], DIMS, preferred_element_type=F32)
    split_units(z, c, rows, keep, send)


def split_units(z, c, rows, keep, send):
    size = keep.shape[1]
    for side, out in ((c, keep), (1 - c, send)):
        for far in range(RING):
            out[far] = rows[side, chunk(z, far, size), :].astype(BF16)


def late_body(place, own, low, partner, block, keep, send, rows, panel):
    z, c = place[0], place[1]
    height = own.shape[0]
    fill(panel, [block])
    rows[0] = partner[...]
    rows[1, :, :height] = lax.dot_general(low[1, height:], panel[0, :height], DIMS, preferred_element_type=F32)
    rows[1, :, height:] = lax.dot_general(own[...], panel[0, :height], DIMS, preferred_element_type=F32)
    split_units(z, c, rows, keep, send)


def panel_body(place, low, *refs):
    *blocks, panel, high = refs
    fill(high, blocks)
    for i in range(2):
        panel[i] = low[i]
        panel[i + 2] = high[i]


def pair_body(place, low, low_other, high, high_other, *outs):
    size = low.shape[1]
    for d in range(RING):
        lower = (low[d].astype(F32) + low_other[d].astype(F32)).astype(BF16)
        upper = (high[d].astype(F32) + high_other[d].astype(F32)).astype(BF16)
        if d == FAR:
            outs[d][...] = lower
            outs[d + 1][...] = upper
        else:
            out = outs[d if d < FAR else d + 1]
            out[:size] = lower
            out[size:] = upper


def add(a, b):
    return (a.astype(F32) + b.astype(F32)).astype(BF16)


def ring_sum(part, up, down):
    size = up.shape[0]
    for step in range(FAR - 1, -1, -1):
        up = shift(up, "z", -1)
        down = shift(down, "z", 1)
        if step == 0:
            total = part[0].astype(F32) + up.astype(F32) + down.astype(F32)
        elif step == FAR - 1:
            one, two = part[step], part[RING - step]
            up = jnp.concatenate([add(one[:size], up), one[size:]], 0)
            down = jnp.concatenate([two[:size], add(two[size:], down)], 0)
        else:
            up, down = add(part[step], up), add(part[RING - step], down)
    return total.astype(BF16)


def group_body(place, *refs):
    *pieces, out = refs
    for i, ref in enumerate(pieces):
        out[i] = ref[...]


def lay(gram, side, group, z):
    size = gram.shape[1] // RING
    for i in range(RING - 1):
        where = chunk(z, i if i < FAR else i + 1, size)
        gram[side, where, :] = group[i, :size]
        gram[side + 2, where, :] = group[i, size:]
    for half in (side, side + 2):
        gram[half, chunk(z, FAR, size), :] = jnp.zeros((size, gram.shape[2]), BF16)


def own_rows_body(place, panel, group, gram, total):
    z, c = place[0], place[1]
    lay(gram, c, group, z)
    total[...] = jnp.zeros(total.shape, F32)

    @pl.loop(0, 2)
    def _(i):
        total[...] += jnp.dot(gram[c + 2 * i], panel[c + 2 * i], preferred_element_type=F32)


def other_rows_body(place, panel, group, before_gram, before, gram, total):
    z, side = place[0], 1 - place[1]
    lay(gram, side, group, z)

    @pl.loop(0, 2)
    def _(i):
        total[...] += jnp.dot(gram[side + 2 * i], panel[side + 2 * i], preferred_element_type=F32)


def update_body(place, own, panel, before_gram, before, mine, other, gram, w_high, w_low, total, acc):
    z, c = place[0], place[1]
    size = gram.shape[1] // RING
    where = chunk(z, FAR, size)
    for side, ref in ((c, mine), (1 - c, other)):
        gram[side, where, :] = ref[:size]
        gram[side + 2, where, :] = ref[size:]
    acc[...] = jnp.zeros(acc.shape, F32)

    @pl.loop(0, 4)
    def _(i):
        acc[...] += jnp.dot(gram[i, where, :], panel[i], preferred_element_type=F32)

    total[...] = before[...]
    total[where, :] = acc[...]
    w = coef_b * own[...].astype(F32) + coef_c * total[...]
    pack(w, w_high)
    w_low[...] = (w - w.astype(BF16).astype(F32)).astype(BF16)


def near_body(place, own, w_low, gram, *refs):
    *blocks, total, panel = refs
    rows = own.shape[0]
    fill(panel, blocks)
    acc = coef_a * own[...].astype(F32)
    total[...] = acc + jnp.dot(gram[0][:, :rows], w_low[...], preferred_element_type=F32)

    @pl.loop(0, 2)
    def _(i):
        total[...] += jnp.dot(gram[i], panel[i], preferred_element_type=F32)


def side_body(place, before, gram, block, total, panel):
    rows = total.shape[0]
    fill(panel, [block])
    total[...] = before[...] + jnp.dot(gram[3][:, rows:], panel[0, :rows], preferred_element_type=F32)


def mid_body(place, before, gram, r11, r31, total, panel):
    fill(panel, (r11, r31))
    total[...] = before[...] + jnp.dot(gram[2], panel[0], preferred_element_type=F32)


def far_body(place, before, gram, r21, out, panel):
    rows, cols = out.shape
    fill(panel, [r21])
    acc = before[...] + jnp.dot(gram[3][:, :rows], panel[0, :rows], preferred_element_type=F32)
    factor = 0.2 * math.sqrt(max(rows * PANEL, cols * math.prod(SIZES[n] for n in COL)))
    out[...] = (acc * factor).astype(BF16)


def newton_step(matrix):
    rows, cols = matrix.shape
    size = rows // RING
    place = jnp.stack([lax.axis_index("z"), lax.axis_index("c")]).astype(jnp.int32)
    width, _, _, height = packing(rows, cols)
    flat = array((rows + height, width))
    block = array((rows, cols))

    packed, own = call(pack_body, place, (matrix,), [flat, block], fixed=False)
    near, r20 = first_blocks(packed)
    part = array((RING, size, 2 * rows))
    wide = array((4, rows, 2 * rows))
    sums = array((rows, cols), F32)
    work = 4 * rows * rows * cols

    def room(count, kind=BF16, width=cols):
        return pltpu.VMEM((count, 2 * rows, width), kind)

    pairs = pltpu.VMEM((2, rows, 2 * rows), F32)
    keep, send, low, partner = call(
        gram_body,
        place,
        (own, packed, *near),
        [part, part, array((2, 2 * rows, cols)), array((rows, 2 * rows), F32)],
        3 * work,
        [pairs, pltpu.VMEM((2 * rows, cols), BF16)],
    )
    halves = [keep, shift(send, "c", 1)]
    keep, send = call(late_body, place, (own, low, partner, r20), [part, part], work, [pairs, room(1)])
    halves += [keep, shift(send, "c", 1)]
    r11, r31, r21 = more_blocks(near, r20, True)
    panel = call(panel_body, place, (low, r11, r31, r21, r20), array((4, 2 * rows, cols)), 0, [room(2)])
    one, two = array((size, 2 * rows)), array((2 * size, 2 * rows))
    parts = call(pair_body, place, halves, [two] * FAR + [one] * 2 + [two] * (FAR - 1))
    part = {d: parts[d if d < FAR else d + 1] for d in range(RING) if d != FAR}
    mine = ring_sum(part, parts[FAR], parts[FAR + 1])
    ahead = mine[size:]
    same = shift(ahead, "yl", 1)
    cross = fetch(ahead, ("yl", "yh"), lambda y, h: (y + 1, h + 1))
    mine = add(mine, shift(mine, "yh", 1))
    ahead = add(same, cross)
    right = lax.broadcasted_iota(jnp.int32, ahead.shape, 1) >= rows
    ahead = jnp.where((place[1] == 1) & right, mine[size:], ahead)
    mine = jnp.concatenate([mine[:size], ahead], 0)

    ring = {0: mine}
    up, down = mine, mine
    for step in range(1, FAR):
        up = shift(up, "z", 1)
        down = shift(down, "z", -1)
        ring[step], ring[RING - step] = up, down
    ends = [shift(up[:size], "z", 1)]
    ends.append(shift(down[size:], "z", -1))
    pieces = [ring[d] for d in range(RING) if d != FAR]
    group = call(group_body, place, pieces, array((RING - 1, 2 * size, 2 * rows)))
    ends = jnp.concatenate(ends, 0)

    other = shift(group, "c", 1)
    gram, total = call(own_rows_body, place, (panel, group), [wide, sums], 2 * work)
    gram, total = call(other_rows_body, place, (panel, other, gram, total), [wide, sums], 2 * work, alias={3: 0, 4: 1})
    gram, w_high, w_low = call(
        update_body,
        place,
        (own, panel, gram, total, ends, shift(ends, "c", 1)),
        [wide, flat, block],
        work // 2,
        [pltpu.VMEM((rows, cols), F32), pltpu.VMEM((size, cols), F32)],
        alias={3: 0},
    )

    near, r20 = first_blocks(w_high)
    ends = more_blocks(near, r20, False)
    total = call(near_body, place, (own, w_low, gram, w_high, *near), sums, 5 * work // 2, [room(2)])
    total = call(side_body, place, (total, gram, r20), sums, work // 2, [room(1)])
    r11, r31, r21 = ends
    total = call(mid_body, place, (total, gram, r11, r31), sums, work, [room(1)])
    return call(far_body, place, (total, gram, r21), block, work // 2, [room(1)], home=True)


def solution(mesh):
    fine = Mesh(mesh.devices.reshape(tuple(SIZES.values())), AXES)
    return jax.shard_map(newton_step, mesh=fine, in_specs=(P(ROW, COL),), out_specs=P(ROW, COL), check_vma=False)
```

```python
import itertools
import math

import jax
import jax.numpy as jnp
from jax import lax
from jax.experimental import pallas as pl
from jax.experimental.pallas import tpu as pltpu
from jax.sharding import Mesh
from jax.sharding import PartitionSpec as P


coef_a = 3.4445
coef_b = -4.775
coef_c = 2.0315


SIZES = {"x": 4, "yl": 2, "z": 8, "yh": 2, "c": 2}
AXES = tuple(SIZES)
ROW = ("x", "yl")
COL = ("z", "yh", "c")
RING = SIZES["z"]
PANEL = SIZES["x"] * SIZES["yl"]
FAR = RING // 2
LANES = 128
VMEM_LIMIT = 14 << 20

F32 = jnp.float32
BF16 = jnp.bfloat16
VMEM = pl.BlockSpec(memory_space=pltpu.VMEM)
SMEM = pl.BlockSpec(memory_space=pltpu.SMEM)


def array(shape, kind=BF16):
    return jax.ShapeDtypeStruct(shape, kind)


def shift(value, axis, step):
    size = SIZES[axis]
    return lax.ppermute(value, axis, [((i + step) % size, i) for i in range(size)])


def fetch(value, axes, source):
    sizes = [SIZES[a] for a in axes]

    def flat(position):
        index = 0
        for p, n in zip(position, sizes, strict=True):
            index = index * n + p % n
        return index

    places = list(itertools.product(*(range(n) for n in sizes)))
    return lax.ppermute(value, axes, [(flat(source(*p)), flat(p)) for p in places])


def call(body, place, operands, outs, flops=0, scratch=(), fixed=True, home=False, alias=None):
    if fixed:
        operands = [pltpu.with_memory_space_constraint(a, pltpu.VMEM) for a in operands]
    single = not isinstance(outs, list)
    outs = [outs] if single else outs
    moved = sum(math.prod(a.shape) * 2 for a in (*operands, *outs))
    got = pl.pallas_call(
        body,
        out_shape=outs if home else [pltpu.VMEM(o.shape, o.dtype) for o in outs],
        in_specs=[SMEM] + [VMEM] * len(operands),
        out_specs=[VMEM] * len(outs),
        scratch_shapes=list(scratch),
        input_output_aliases=alias or {},
        cost_estimate=pl.CostEstimate(flops=flops, bytes_accessed=moved, transcendentals=0),
        compiler_params=pltpu.CompilerParams(vmem_limit_bytes=VMEM_LIMIT),
    )(place, *operands)
    return got[0] if single else got


def near_blocks(own):
    return lax.optimization_barrier((shift(own, "x", 1), shift(own, "x", -1), shift(own, "yl", 1)))


def halves_of(near_up, near_down):
    half = (near_up.shape[0] // 2 + 15) // 16 * 16
    first = shift(near_up[:half], "x", 1)
    return first, shift(near_down[half:], "x", -1)


def packing(rows, cols):
    width = cols // LANES * LANES
    rest = cols - width
    groups = width // rest
    return width, rest, groups, rows // groups


def pack(block, out):
    rows, cols = block.shape
    width, rest, groups, height = packing(rows, cols)
    out[:rows] = block[:, :width].astype(BF16)
    for g in range(groups):
        out[rows:, g * rest : (g + 1) * rest] = block[g * height : (g + 1) * height, width:].astype(BF16)


def fill(panel, refs):
    half, cols = panel.shape[1:]
    rows = half // 2
    width, rest, groups, height = packing(rows, cols)
    total = rows + height
    at = 0
    for ref in refs:
        size = ref.shape[0]
        block, begin = divmod(at, total)
        i, base = divmod(block * rows, half)
        main = min(size, rows - begin)
        panel[i, base + begin : base + begin + main, :width] = ref[:main]
        if begin + size == total:
            for g in range(groups):
                low = base + g * height
                panel[i, low : low + height, width:] = ref[main:, g * rest : (g + 1) * rest]
        at += size


def pack_body(place, own, packed, copy):
    value = own[...]
    copy[...] = value
    pack(value.astype(F32), packed)


def chunk(z, far, size):
    return pl.ds(pl.multiple_of(lax.rem(z + far, RING) * size, 8), size)


DIMS = (((1,), (1,)), ((), ()))


def gram_body(place, own, *refs):
    *blocks, keep, send, panel, partner, rows, left = refs
    fill(panel, blocks)
    z, c = place[0], place[1]
    height = own.shape[0]
    panel[2, :height] = panel[0, height:]
    panel[2, height:] = panel[1, :height]
    left[0], left[1] = own[...], panel[1, height:]

    @pl.loop(0, 3)
    def _(i):
        rows[i] = lax.dot_general(left[jnp.where(i == 2, 1, 0)], panel[i], DIMS, preferred_element_type=F32)

    partner[...] = rows[2]
    split_units(z, c, rows, keep, send)


def split_units(z, c, rows, keep, send):
    size = keep.shape[1]

    @pl.loop(0, RING)
    def _(far):
        for side, out in ((c, keep), (1 - c, send)):
            out[far] = rows[side, chunk(z, far, size), :].astype(BF16)


def late_body(place, own, low, partner, top, bottom, keep, send, rows, panel, left, blocks):
    z, c = place[0], place[1]
    height = own.shape[0]
    fill(panel, [top, bottom])
    rows[0] = partner[...]
    left[0], left[1] = low[1, height:], own[...]

    @pl.loop(0, 2)
    def _(i):
        blocks[i] = lax.dot_general(left[i], panel[0, :height], DIMS, preferred_element_type=F32)

    rows[1, :, :height] = blocks[0]
    rows[1, :, height:] = blocks[1]
    split_units(z, c, rows, keep, send)


def panel_body(place, low, *refs):
    *blocks, panel, high = refs
    fill(high, blocks)

    @pl.loop(0, 2)
    def _(i):
        panel[i] = low[i]
        panel[i + 2] = high[i]


def pair_body(place, low, low_other, high, high_other, *outs):
    size = low.shape[1]
    for d in range(RING):
        lower = (low[d].astype(F32) + low_other[d].astype(F32)).astype(BF16)
        upper = (high[d].astype(F32) + high_other[d].astype(F32)).astype(BF16)
        if d == FAR:
            outs[d][...] = lower
            outs[d + 1][...] = upper
        else:
            out = outs[d if d < FAR else d + 1]
            out[:size] = lower
            out[size:] = upper


def add(a, b):
    return (a.astype(F32) + b.astype(F32)).astype(BF16)


def ring_sum(part, up, down):
    size = up.shape[0]
    for step in range(FAR - 1, -1, -1):
        up = shift(up, "z", -1)
        down = shift(down, "z", 1)
        if step == 0:
            total = part[0].astype(F32) + up.astype(F32) + down.astype(F32)
        elif step == FAR - 1:
            one, two = part[step], part[RING - step]
            up = jnp.concatenate([add(one[:size], up), one[size:]], 0)
            down = jnp.concatenate([two[:size], add(two[size:], down)], 0)
        else:
            up, down = add(part[step], up), add(part[RING - step], down)
    return total.astype(BF16)


def group_body(place, *refs):
    *pieces, out = refs
    for i, ref in enumerate(pieces):
        out[i] = ref[...]


def lay(gram, side, group, z):
    size = gram.shape[1] // RING

    @pl.loop(0, RING - 1)
    def _(i):
        where = chunk(z, i + jnp.where(i >= FAR, 1, 0), size)
        gram[side, where, :] = group[i, :size]
        gram[side + 2, where, :] = group[i, size:]

    @pl.loop(0, 2)
    def _(i):
        gram[side + 2 * i, chunk(z, FAR, size), :] = jnp.zeros((size, gram.shape[2]), BF16)


def own_rows_body(place, panel, group, gram, total):
    z, c = place[0], place[1]
    lay(gram, c, group, z)
    total[...] = jnp.zeros(total.shape, F32)

    @pl.loop(0, 2)
    def _(i):
        total[...] += jnp.dot(gram[c + 2 * i], panel[c + 2 * i], preferred_element_type=F32)


def other_rows_body(place, panel, group, before_gram, before, gram, total):
    z, side = place[0], 1 - place[1]
    lay(gram, side, group, z)

    @pl.loop(0, 2)
    def _(i):
        total[...] += jnp.dot(gram[side + 2 * i], panel[side + 2 * i], preferred_element_type=F32)


def update_body(place, own, panel, before_gram, before, mine, other, gram, w_high, w_low, total, acc):
    z, c = place[0], place[1]
    size = gram.shape[1] // RING
    where = chunk(z, FAR, size)
    for side, ref in ((c, mine), (1 - c, other)):
        gram[side, where, :] = ref[:size]
        gram[side + 2, where, :] = ref[size:]
    acc[...] = jnp.zeros(acc.shape, F32)

    @pl.loop(0, 4)
    def _(i):
        acc[...] += jnp.dot(gram[i, where, :], panel[i], preferred_element_type=F32)

    total[...] = before[...]
    total[where, :] = acc[...]
    w = coef_b * own[...].astype(F32) + coef_c * total[...]
    pack(w, w_high)
    w_low[...] = (w - w.astype(BF16).astype(F32)).astype(BF16)


def near_body(place, own, w_low, gram, *refs):
    *blocks, total, panel = refs
    rows = own.shape[0]
    fill(panel, blocks)
    acc = coef_a * own[...].astype(F32)
    total[...] = acc + jnp.dot(gram[0][:, :rows], w_low[...], preferred_element_type=F32)

    @pl.loop(0, 2)
    def _(i):
        total[...] += jnp.dot(gram[i], panel[i], preferred_element_type=F32)


def side_body(place, before, gram, r11, r31, total, panel):
    fill(panel, (r11, r31))
    total[...] = before[...] + jnp.dot(gram[2], panel[0], preferred_element_type=F32)


def far_body(place, before, gram, *refs):
    *blocks, out, panel = refs
    rows, cols = out.shape
    fill(panel, blocks)
    acc = before[...] + jnp.dot(gram[3], panel[0], preferred_element_type=F32)
    factor = 0.2 * math.sqrt(max(rows * PANEL, cols * math.prod(SIZES[n] for n in COL)))
    out[...] = (acc * factor).astype(BF16)


def newton_step(matrix):
    rows, cols = matrix.shape
    size = rows // RING
    place = jnp.stack([lax.axis_index("z"), lax.axis_index("c")]).astype(jnp.int32)
    width, _, _, height = packing(rows, cols)
    flat = array((rows + height, width))
    block = array((rows, cols))

    packed, own = call(pack_body, place, (matrix,), [flat, block], fixed=False)
    near = near_blocks(packed)
    r20 = halves_of(near[0], near[1])
    part = array((RING, size, 2 * rows))
    wide = array((4, rows, 2 * rows))
    sums = array((rows, cols), F32)
    work = 4 * rows * rows * cols

    def room(count, kind=BF16, width=cols):
        return pltpu.VMEM((count, 2 * rows, width), kind)

    pairs = pltpu.VMEM((2, rows, 2 * rows), F32)
    keep, send, low, partner = call(
        gram_body,
        place,
        (own, packed, *near),
        [part, part, array((3, 2 * rows, cols)), array((rows, 2 * rows), F32)],
        3 * work,
        [pltpu.VMEM((3, rows, 2 * rows), F32), pltpu.VMEM((2, rows, cols), BF16)],
    )
    halves = [keep, shift(send, "c", 1)]
    scratch = [pairs, room(1), pltpu.VMEM((2, rows, cols), BF16), pltpu.VMEM((2, rows, rows), F32)]
    keep, send = call(late_body, place, (own, low, partner, *r20), [part, part], work, scratch)
    halves += [keep, shift(send, "c", 1)]
    r11 = shift(near[2], "x", 1)
    r31 = shift(near[2], "x", -1)
    r21 = shift(jnp.concatenate(r20, 0), "yl", 1)
    panel = call(panel_body, place, (low, r11, r31, r21, *r20), array((4, 2 * rows, cols)), 0, [room(2)])
    one, two = array((size, 2 * rows)), array((2 * size, 2 * rows))
    parts = call(pair_body, place, halves, [two] * FAR + [one] * 2 + [two] * (FAR - 1))
    part = {d: parts[d if d < FAR else d + 1] for d in range(RING) if d != FAR}
    mine = ring_sum(part, parts[FAR], parts[FAR + 1])
    ahead = mine[size:]
    same = shift(ahead, "yl", 1)
    cross = fetch(ahead, ("yl", "yh"), lambda y, h: (y + 1, h + 1))
    mine = add(mine, shift(mine, "yh", 1))
    ahead = add(same, cross)
    right = lax.broadcasted_iota(jnp.int32, ahead.shape, 1) >= rows
    ahead = jnp.where((place[1] == 1) & right, mine[size:], ahead)
    mine = jnp.concatenate([mine[:size], ahead], 0)

    ring = {0: mine}
    up, down = mine, mine
    for step in range(1, FAR):
        up = shift(up, "z", 1)
        down = shift(down, "z", -1)
        ring[step], ring[RING - step] = up, down
    ends = [shift(up[:size], "z", 1)]
    ends.append(shift(down[size:], "z", -1))
    pieces = [ring[d] for d in range(RING) if d != FAR]
    group = call(group_body, place, pieces, array((RING - 1, 2 * size, 2 * rows)))
    ends = jnp.concatenate(ends, 0)

    other = shift(group, "c", 1)
    gram, total = call(own_rows_body, place, (panel, group), [wide, sums], 2 * work)
    gram, total = call(other_rows_body, place, (panel, other, gram, total), [wide, sums], 2 * work, alias={3: 0, 4: 1})
    gram, w_high, w_low = call(
        update_body,
        place,
        (own, panel, gram, total, ends, shift(ends, "c", 1)),
        [wide, flat, block],
        work // 2,
        [pltpu.VMEM((rows, cols), F32), pltpu.VMEM((size, cols), F32)],
        alias={3: 0},
    )

    near = near_blocks(w_high)
    total = call(near_body, place, (own, w_low, gram, w_high, *near), sums, 5 * work // 2, [room(2)])
    _, r30, r01 = near
    r20, r11, r31 = lax.optimization_barrier((shift(r30, "x", -1), shift(r01, "x", 1), shift(r30, "yl", 1)))
    total = call(side_body, place, (total, gram, r11, r31), sums, work, [room(1)])
    r21 = halves_of(r11, r31)
    return call(far_body, place, (total, gram, *r21, r20), block, work, [room(1)], home=True)


def solution(mesh):
    fine = Mesh(mesh.devices.reshape(tuple(SIZES.values())), AXES)
    return jax.shard_map(newton_step, mesh=fine, in_specs=(P(ROW, COL),), out_specs=P(ROW, COL), check_vma=False)
```

```python
import itertools
import math

import jax
import jax.numpy as jnp
from jax import lax
from jax.experimental import pallas as pl
from jax.experimental.pallas import tpu as pltpu
from jax.sharding import Mesh
from jax.sharding import PartitionSpec as P


coef_a = 3.4445
coef_b = -4.775
coef_c = 2.0315


SIZES = {"x": 4, "yl": 2, "z": 8, "yh": 2, "c": 2}
AXES = tuple(SIZES)
ROW = ("x", "yl")
COL = ("z", "yh", "c")
RING = SIZES["z"]
PANEL = SIZES["x"] * SIZES["yl"]
FAR = RING // 2
LANES = 128
VMEM_LIMIT = 14 << 20

F32 = jnp.float32
BF16 = jnp.bfloat16
VMEM = pl.BlockSpec(memory_space=pltpu.VMEM)
SMEM = pl.BlockSpec(memory_space=pltpu.SMEM)


def array(shape, kind=BF16):
    return jax.ShapeDtypeStruct(shape, kind)


def shift(value, axis, step):
    size = SIZES[axis]
    return lax.ppermute(value, axis, [((i + step) % size, i) for i in range(size)])


def fetch(value, axes, source):
    sizes = [SIZES[a] for a in axes]

    def flat(position):
        index = 0
        for p, n in zip(position, sizes, strict=True):
            index = index * n + p % n
        return index

    places = list(itertools.product(*(range(n) for n in sizes)))
    return lax.ppermute(value, axes, [(flat(source(*p)), flat(p)) for p in places])


def call(body, place, operands, outs, flops=0, scratch=(), fixed=True, home=False, alias=None):
    if fixed:
        operands = [pltpu.with_memory_space_constraint(a, pltpu.VMEM) for a in operands]
    single = not isinstance(outs, list)
    outs = [outs] if single else outs
    moved = sum(math.prod(a.shape) * 2 for a in (*operands, *outs))
    got = pl.pallas_call(
        body,
        out_shape=outs if home else [pltpu.VMEM(o.shape, o.dtype) for o in outs],
        in_specs=[SMEM] + [VMEM] * len(operands),
        out_specs=[VMEM] * len(outs),
        scratch_shapes=list(scratch),
        input_output_aliases=alias or {},
        cost_estimate=pl.CostEstimate(flops=flops, bytes_accessed=moved, transcendentals=0),
        compiler_params=pltpu.CompilerParams(vmem_limit_bytes=VMEM_LIMIT),
    )(place, *operands)
    return got[0] if single else got


def near_blocks(own):
    return lax.optimization_barrier((shift(own, "x", 1), shift(own, "x", -1), shift(own, "yl", 1)))


def halves_of(near_up, near_down):
    half = (near_up.shape[0] // 2 + 15) // 16 * 16
    first = shift(near_up[:half], "x", 1)
    return first, shift(near_down[half:], "x", -1)


def packing(rows, cols):
    width = cols // LANES * LANES
    rest = cols - width
    groups = width // rest
    return width, rest, groups, rows // groups


def pack(block, out):
    rows, cols = block.shape
    width, rest, groups, height = packing(rows, cols)
    out[:rows] = block[:, :width].astype(BF16)
    for g in range(groups):
        out[rows:, g * rest : (g + 1) * rest] = block[g * height : (g + 1) * height, width:].astype(BF16)


def copy_rows(panel, i, begin, ref, rows, width):
    step = math.gcd(math.gcd(rows, begin), 64)

    @pl.loop(0, rows // step)
    def _(k):
        at = pl.multiple_of(k * step, step)
        panel[i, pl.ds(begin + at, step), :width] = ref[pl.ds(at, step), :]


def fill(panel, refs):
    half, cols = panel.shape[1:]
    rows = half // 2
    width, rest, groups, height = packing(rows, cols)
    total = rows + height
    at = 0
    for ref in refs:
        size = ref.shape[0]
        block, begin = divmod(at, total)
        i, base = divmod(block * rows, half)
        main = min(size, rows - begin)
        copy_rows(panel, i, base + begin, ref, main, width)
        if begin + size == total:
            for g in range(groups):
                low = base + g * height
                panel[i, low : low + height, width:] = ref[main:, g * rest : (g + 1) * rest]
        at += size


def pack_body(place, own, packed, copy):
    value = own[...]
    copy[...] = value
    pack(value.astype(F32), packed)


def chunk(z, far, size):
    return pl.ds(pl.multiple_of(lax.rem(z + far, RING) * size, 8), size)


DIMS = (((1,), (1,)), ((), ()))


def gram_body(place, own, *refs):
    *blocks, keep, send, panel, partner, rows, left = refs
    fill(panel, blocks)
    z, c = place[0], place[1]
    height = own.shape[0]
    panel[2, :height] = panel[0, height:]
    panel[2, height:] = panel[1, :height]
    left[0], left[1] = own[...], panel[1, height:]

    @pl.loop(0, 3)
    def _(i):
        rows[i] = lax.dot_general(left[jnp.where(i == 2, 1, 0)], panel[i], DIMS, preferred_element_type=F32)

    partner[...] = rows[2]
    split_units(z, c, rows, keep, send)


def split_units(z, c, rows, keep, send):
    size = keep.shape[1]

    @pl.loop(0, RING)
    def _(far):
        for side, out in ((c, keep), (1 - c, send)):
            out[far] = rows[side, chunk(z, far, size), :].astype(BF16)


def late_body(place, own, low, partner, top, bottom, keep, send, rows, panel, left, blocks):
    z, c = place[0], place[1]
    height = own.shape[0]
    fill(panel, [top, bottom])
    rows[0] = partner[...]
    left[0], left[1] = low[1, height:], own[...]

    @pl.loop(0, 2)
    def _(i):
        blocks[i] = lax.dot_general(left[i], panel[0, :height], DIMS, preferred_element_type=F32)

    rows[1, :, :height] = blocks[0]
    rows[1, :, height:] = blocks[1]
    split_units(z, c, rows, keep, send)


def panel_body(place, low, *refs):
    *blocks, panel, high = refs
    fill(high, blocks)

    @pl.loop(0, 2)
    def _(i):
        panel[i] = low[i]
        panel[i + 2] = high[i]


def pair_body(place, low, low_other, high, high_other, *outs):
    size = low.shape[1]
    for d in range(RING):
        lower = (low[d].astype(F32) + low_other[d].astype(F32)).astype(BF16)
        upper = (high[d].astype(F32) + high_other[d].astype(F32)).astype(BF16)
        if d == FAR:
            outs[d][...] = lower
            outs[d + 1][...] = upper
        else:
            out = outs[d if d < FAR else d + 1]
            out[:size] = lower
            out[size:] = upper


def add(a, b):
    return (a.astype(F32) + b.astype(F32)).astype(BF16)


def ring_sum(part, up, down):
    size = up.shape[0]
    for step in range(FAR - 1, -1, -1):
        up = shift(up, "z", -1)
        down = shift(down, "z", 1)
        if step == 0:
            total = part[0].astype(F32) + up.astype(F32) + down.astype(F32)
        elif step == FAR - 1:
            one, two = part[step], part[RING - step]
            up = jnp.concatenate([add(one[:size], up), one[size:]], 0)
            down = jnp.concatenate([two[:size], add(two[size:], down)], 0)
        else:
            up, down = add(part[step], up), add(part[RING - step], down)
    return total.astype(BF16)


def group_body(place, *refs):
    *pieces, out = refs
    for i, ref in enumerate(pieces):
        out[i] = ref[...]


def lay(gram, side, group, z):
    size = gram.shape[1] // RING

    @pl.loop(0, RING - 1)
    def _(i):
        where = chunk(z, i + jnp.where(i >= FAR, 1, 0), size)
        gram[side, where, :] = group[i, :size]
        gram[side + 2, where, :] = group[i, size:]

    @pl.loop(0, 2)
    def _(i):
        gram[side + 2 * i, chunk(z, FAR, size), :] = jnp.zeros((size, gram.shape[2]), BF16)


def own_rows_body(place, panel, group, gram, total):
    z, c = place[0], place[1]
    lay(gram, c, group, z)
    total[...] = jnp.zeros(total.shape, F32)

    @pl.loop(0, 2)
    def _(i):
        total[...] += jnp.dot(gram[c + 2 * i], panel[c + 2 * i], preferred_element_type=F32)


def other_rows_body(place, panel, group, before_gram, before, gram, total):
    z, side = place[0], 1 - place[1]
    lay(gram, side, group, z)

    @pl.loop(0, 2)
    def _(i):
        total[...] += jnp.dot(gram[side + 2 * i], panel[side + 2 * i], preferred_element_type=F32)


def update_body(place, own, panel, before_gram, before, mine, other, gram, w_high, w_low, total, acc):
    z, c = place[0], place[1]
    size = gram.shape[1] // RING
    where = chunk(z, FAR, size)
    for side, ref in ((c, mine), (1 - c, other)):
        gram[side, where, :] = ref[:size]
        gram[side + 2, where, :] = ref[size:]
    acc[...] = jnp.zeros(acc.shape, F32)

    @pl.loop(0, 4)
    def _(i):
        acc[...] += jnp.dot(gram[i, where, :], panel[i], preferred_element_type=F32)

    total[...] = before[...]
    total[where, :] = acc[...]
    w = coef_b * own[...].astype(F32) + coef_c * total[...]
    pack(w, w_high)
    w_low[...] = (w - w.astype(BF16).astype(F32)).astype(BF16)


def near_body(place, own, w_low, gram, *refs):
    *blocks, total, panel = refs
    rows = own.shape[0]
    fill(panel, blocks)
    panel[3, :rows] = w_low[...]
    panel[3, rows:] = jnp.zeros((rows, own.shape[1]), BF16)
    total[...] = coef_a * own[...].astype(F32)

    @pl.loop(0, 4)
    def _(i):
        total[...] += jnp.dot(gram[jnp.where(i == 3, 0, i)], panel[i], preferred_element_type=F32)


def far_body(place, before, gram, *refs):
    *blocks, out, panel = refs
    rows, cols = out.shape
    fill(panel, blocks)
    acc = before[...] + jnp.dot(gram[3], panel[0], preferred_element_type=F32)
    factor = 0.2 * math.sqrt(max(rows * PANEL, cols * math.prod(SIZES[n] for n in COL)))
    out[...] = (acc * factor).astype(BF16)


def newton_step(matrix):
    rows, cols = matrix.shape
    size = rows // RING
    place = jnp.stack([lax.axis_index("z"), lax.axis_index("c")]).astype(jnp.int32)
    width, _, _, height = packing(rows, cols)
    flat = array((rows + height, width))
    block = array((rows, cols))

    packed, own = call(pack_body, place, (matrix,), [flat, block], fixed=False)
    near = near_blocks(packed)
    r20 = halves_of(near[0], near[1])
    part = array((RING, size, 2 * rows))
    wide = array((4, rows, 2 * rows))
    sums = array((rows, cols), F32)
    work = 4 * rows * rows * cols

    def room(count, kind=BF16, width=cols):
        return pltpu.VMEM((count, 2 * rows, width), kind)

    pairs = pltpu.VMEM((2, rows, 2 * rows), F32)
    keep, send, low, partner = call(
        gram_body,
        place,
        (own, packed, *near),
        [part, part, array((3, 2 * rows, cols)), array((rows, 2 * rows), F32)],
        3 * work,
        [pltpu.VMEM((3, rows, 2 * rows), F32), pltpu.VMEM((2, rows, cols), BF16)],
    )
    halves = [keep, shift(send, "c", 1)]
    scratch = [pairs, room(1), pltpu.VMEM((2, rows, cols), BF16), pltpu.VMEM((2, rows, rows), F32)]
    keep, send = call(late_body, place, (own, low, partner, *r20), [part, part], work, scratch)
    halves += [keep, shift(send, "c", 1)]
    r11 = shift(near[2], "x", 1)
    r31 = shift(near[2], "x", -1)
    r21 = shift(jnp.concatenate(r20, 0), "yl", 1)
    panel = call(panel_body, place, (low, r11, r31, r21, *r20), array((4, 2 * rows, cols)), 0, [room(2)])
    one, two = array((size, 2 * rows)), array((2 * size, 2 * rows))
    parts = call(pair_body, place, halves, [two] * FAR + [one] * 2 + [two] * (FAR - 1))
    part = {d: parts[d if d < FAR else d + 1] for d in range(RING) if d != FAR}
    mine = ring_sum(part, parts[FAR], parts[FAR + 1])
    ahead = mine[size:]
    same = shift(ahead, "yl", 1)
    cross = fetch(ahead, ("yl", "yh"), lambda y, h: (y + 1, h + 1))
    mine = add(mine, shift(mine, "yh", 1))
    ahead = add(same, cross)
    right = lax.broadcasted_iota(jnp.int32, ahead.shape, 1) >= rows
    ahead = jnp.where((place[1] == 1) & right, mine[size:], ahead)
    mine = jnp.concatenate([mine[:size], ahead], 0)

    ring = {0: mine}
    up, down = mine, mine
    for step in range(1, FAR):
        up = shift(up, "z", 1)
        down = shift(down, "z", -1)
        ring[step], ring[RING - step] = up, down
    ends = [shift(up[:size], "z", 1)]
    ends.append(shift(down[size:], "z", -1))
    pieces = [ring[d] for d in range(RING) if d != FAR]
    group = call(group_body, place, pieces, array((RING - 1, 2 * size, 2 * rows)))
    ends = jnp.concatenate(ends, 0)

    other = shift(group, "c", 1)
    gram, total = call(own_rows_body, place, (panel, group), [wide, sums], 2 * work)
    gram, total = call(other_rows_body, place, (panel, other, gram, total), [wide, sums], 2 * work, alias={3: 0, 4: 1})
    gram, w_high, w_low = call(
        update_body,
        place,
        (own, panel, gram, total, ends, shift(ends, "c", 1)),
        [wide, flat, block],
        work // 2,
        [pltpu.VMEM((rows, cols), F32), pltpu.VMEM((size, cols), F32)],
        alias={3: 0},
    )

    near = near_blocks(w_high)
    _, r30, r01 = near
    r20, r11, r31 = lax.optimization_barrier((shift(r30, "x", -1), shift(r01, "x", 1), shift(r30, "yl", 1)))
    blocks = (own, w_low, gram, w_high, *near, r11, r31)
    total = call(near_body, place, blocks, sums, 4 * work, [room(4)])
    r21 = halves_of(r11, r31)
    return call(far_body, place, (total, gram, *r21, r20), block, work, [room(1)], home=True)


def solution(mesh):
    fine = Mesh(mesh.devices.reshape(tuple(SIZES.values())), AXES)
    return jax.shard_map(newton_step, mesh=fine, in_specs=(P(ROW, COL),), out_specs=P(ROW, COL), check_vma=False)
```

```python
import itertools
import math

import jax
import jax.numpy as jnp
from jax import lax
from jax.experimental import pallas as pl
from jax.experimental.pallas import tpu as pltpu
from jax.sharding import Mesh
from jax.sharding import PartitionSpec as P


coef_a = 3.4445
coef_b = -4.775
coef_c = 2.0315


SIZES = {"x": 4, "yl": 2, "z": 8, "yh": 2, "c": 2}
AXES = tuple(SIZES)
ROW = ("x", "yl")
COL = ("z", "yh", "c")
RING = SIZES["z"]
PANEL = SIZES["x"] * SIZES["yl"]
FAR = RING // 2
LANES = 128
VMEM_LIMIT = 14 << 20

F32 = jnp.float32
BF16 = jnp.bfloat16
VMEM = pl.BlockSpec(memory_space=pltpu.VMEM)
SMEM = pl.BlockSpec(memory_space=pltpu.SMEM)


def array(shape, kind=BF16):
    return jax.ShapeDtypeStruct(shape, kind)


def shift(value, axis, step):
    size = SIZES[axis]
    return lax.ppermute(value, axis, [((i + step) % size, i) for i in range(size)])


def fetch(value, axes, source):
    sizes = [SIZES[a] for a in axes]

    def flat(position):
        index = 0
        for p, n in zip(position, sizes, strict=True):
            index = index * n + p % n
        return index

    places = list(itertools.product(*(range(n) for n in sizes)))
    return lax.ppermute(value, axes, [(flat(source(*p)), flat(p)) for p in places])


def call(body, place, operands, outs, flops=0, scratch=(), fixed=True, home=False, alias=None):
    if fixed:
        operands = [pltpu.with_memory_space_constraint(a, pltpu.VMEM) for a in operands]
    single = not isinstance(outs, list)
    outs = [outs] if single else outs
    moved = sum(math.prod(a.shape) * 2 for a in (*operands, *outs))
    got = pl.pallas_call(
        body,
        out_shape=outs if home else [pltpu.VMEM(o.shape, o.dtype) for o in outs],
        in_specs=[SMEM] + [VMEM] * len(operands),
        out_specs=[VMEM] * len(outs),
        scratch_shapes=list(scratch),
        input_output_aliases=alias or {},
        cost_estimate=pl.CostEstimate(flops=flops, bytes_accessed=moved, transcendentals=0),
        compiler_params=pltpu.CompilerParams(vmem_limit_bytes=VMEM_LIMIT),
    )(place, *operands)
    return got[0] if single else got


def near_blocks(own):
    return lax.optimization_barrier((shift(own, "x", 1), shift(own, "x", -1), shift(own, "yl", 1)))


def halves_of(near_up, near_down):
    half = (near_up.shape[0] // 2 + 15) // 16 * 16
    first = shift(near_up[:half], "x", 1)
    return first, shift(near_down[half:], "x", -1)


def packing(rows, cols):
    width = cols // LANES * LANES
    rest = cols - width
    groups = width // rest
    return width, rest, groups, rows // groups


def pack(block, out):
    rows, cols = block.shape
    width, rest, groups, height = packing(rows, cols)
    out[:rows] = block[:, :width].astype(BF16)
    for g in range(groups):
        out[rows:, g * rest : (g + 1) * rest] = block[g * height : (g + 1) * height, width:].astype(BF16)


def copy_rows(panel, i, begin, ref, rows, width):
    step = math.gcd(math.gcd(rows, begin), 64)

    @pl.loop(0, rows // step)
    def _(k):
        at = pl.multiple_of(k * step, step)
        panel[i, pl.ds(begin + at, step), :width] = ref[pl.ds(at, step), :]


def fill(panel, refs, skip=0):
    half, cols = panel.shape[1:]
    rows = half // 2
    width, rest, groups, height = packing(rows, cols)
    total = rows + height
    at = skip * total
    for ref in refs:
        size = ref.shape[0]
        block, begin = divmod(at, total)
        i, base = divmod(block * rows, half)
        main = min(size, rows - begin)
        copy_rows(panel, i, base + begin, ref, main, width)
        if begin + size == total:
            for g in range(groups):
                low = base + g * height
                panel[i, low : low + height, width:] = ref[main:, g * rest : (g + 1) * rest]
        at += size


def pack_body(place, own, packed, copy):
    value = own[...]
    copy[...] = value
    pack(value.astype(F32), packed)


def chunk(z, far, size):
    return pl.ds(pl.multiple_of(lax.rem(z + far, RING) * size, 8), size)


DIMS = (((1,), (1,)), ((), ()))


def gram_body(place, own, *refs):
    *blocks, keep, send, panel, partner, rows, left = refs
    fill(panel, blocks)
    z, c = place[0], place[1]
    height = own.shape[0]
    panel[2, :height] = panel[0, height:]
    panel[2, height:] = panel[1, :height]
    left[0], left[1] = own[...], panel[1, height:]

    @pl.loop(0, 3)
    def _(i):
        rows[i] = lax.dot_general(left[jnp.where(i == 2, 1, 0)], panel[i], DIMS, preferred_element_type=F32)

    partner[...] = rows[2]
    split_units(z, c, rows, keep, send)


def split_units(z, c, rows, keep, send):
    size = keep.shape[1]

    @pl.loop(0, RING)
    def _(far):
        for side, out in ((c, keep), (1 - c, send)):
            out[far] = rows[side, chunk(z, far, size), :].astype(BF16)


def late_body(place, own, low, partner, top, bottom, keep, send, rows, panel, left, blocks):
    z, c = place[0], place[1]
    height = own.shape[0]
    fill(panel, [top, bottom])
    rows[0] = partner[...]
    left[0], left[1] = low[1, height:], own[...]

    @pl.loop(0, 2)
    def _(i):
        blocks[i] = lax.dot_general(left[i], panel[0, :height], DIMS, preferred_element_type=F32)

    rows[1, :, :height] = blocks[0]
    rows[1, :, height:] = blocks[1]
    split_units(z, c, rows, keep, send)


def panel_body(place, low, *refs):
    *blocks, panel, high = refs
    fill(high, blocks)

    @pl.loop(0, 2)
    def _(i):
        panel[i] = low[i]
        panel[i + 2] = high[i]


def pair_body(place, low, low_other, high, high_other, *outs):
    size = low.shape[1]
    for d in range(RING):
        lower = (low[d].astype(F32) + low_other[d].astype(F32)).astype(BF16)
        upper = (high[d].astype(F32) + high_other[d].astype(F32)).astype(BF16)
        if d == FAR:
            outs[d][...] = lower
            outs[d + 1][...] = upper
        else:
            out = outs[d if d < FAR else d + 1]
            out[:size] = lower
            out[size:] = upper


def add(a, b):
    return (a.astype(F32) + b.astype(F32)).astype(BF16)


def ring_sum(place, part, up, down):
    size = up.shape[0]
    for step in range(FAR - 1, -1, -1):
        up = shift(up, "z", -1)
        down = shift(down, "z", 1)
        if step == 0:
            return call(sum_body, place, (part[0], up, down), [array(part[0].shape), array((size, up.shape[1]))])
        elif step == FAR - 1:
            one, two = part[step], part[RING - step]
            up = jnp.concatenate([add(one[:size], up), one[size:]], 0)
            down = jnp.concatenate([two[:size], add(two[size:], down)], 0)
        else:
            up, down = add(part[step], up), add(part[RING - step], down)


def sum_body(place, near, up, down, mine, ahead):
    size = ahead.shape[0]
    total = near[...].astype(F32) + up[...].astype(F32) + down[...].astype(F32)
    mine[...] = total.astype(BF16)
    ahead[...] = total[size:].astype(BF16)


def join_body(place, mine, across, same, cross, out):
    size, width = same.shape
    own = mine[...].astype(F32) + across[...].astype(F32)
    ahead = same[...].astype(F32) + cross[...].astype(F32)
    right = lax.broadcasted_iota(jnp.int32, (size, width), 1) >= width // 2
    out[:size] = own[:size].astype(BF16)
    out[size:] = jnp.where(right & (place[1] == 1), own[size:], ahead).astype(BF16)


def group_body(place, *refs):
    *pieces, out = refs
    for i, ref in enumerate(pieces):
        out[i] = ref[...]


def lay(gram, side, group, z):
    size = gram.shape[1] // RING

    @pl.loop(0, RING - 1)
    def _(i):
        where = chunk(z, i + jnp.where(i >= FAR, 1, 0), size)
        gram[side, where, :] = group[i, :size]
        gram[side + 2, where, :] = group[i, size:]

    @pl.loop(0, 2)
    def _(i):
        gram[side + 2 * i, chunk(z, FAR, size), :] = jnp.zeros((size, gram.shape[2]), BF16)


def own_rows_body(place, panel, group, gram, total):
    z, c = place[0], place[1]
    lay(gram, c, group, z)
    total[...] = jnp.zeros(total.shape, F32)

    @pl.loop(0, 2)
    def _(i):
        total[...] += jnp.dot(gram[c + 2 * i], panel[c + 2 * i], preferred_element_type=F32)


def other_rows_body(place, panel, group, before_gram, before, gram, total):
    z, side = place[0], 1 - place[1]
    lay(gram, side, group, z)

    @pl.loop(0, 2)
    def _(i):
        total[...] += jnp.dot(gram[side + 2 * i], panel[side + 2 * i], preferred_element_type=F32)


def update_body(place, own, panel, before_gram, before, mine, other, gram, w_high, w_low, total, acc):
    z, c = place[0], place[1]
    size = gram.shape[1] // RING
    where = chunk(z, FAR, size)
    for side, ref in ((c, mine), (1 - c, other)):
        gram[side, where, :] = ref[:size]
        gram[side + 2, where, :] = ref[size:]
    acc[...] = jnp.zeros(acc.shape, F32)

    @pl.loop(0, 4)
    def _(i):
        acc[...] += jnp.dot(gram[i, where, :], panel[i], preferred_element_type=F32)

    total[...] = before[...]
    total[where, :] = acc[...]
    w = coef_b * own[...].astype(F32) + coef_c * total[...]
    pack(w, w_high)
    w_low[...] = (w - w.astype(BF16).astype(F32)).astype(BF16)


def near_body(place, own, w_low, gram, *refs):
    *blocks, r20, total, panel = refs
    rows = own.shape[0]
    fill(panel, blocks)
    fill(panel, [r20], 9)
    panel[3, :rows] = w_low[...]
    panel[3, rows:] = jnp.zeros((rows, own.shape[1]), BF16)
    panel[4, :rows] = jnp.zeros((rows, own.shape[1]), BF16)
    total[...] = coef_a * own[...].astype(F32)

    @pl.loop(0, 5)
    def _(i):
        side = jnp.where(i == 3, 0, jnp.minimum(i, 3))
        total[...] += jnp.dot(gram[side], panel[i], preferred_element_type=F32)


def far_body(place, before, gram, *refs):
    *pieces, out, panel = refs
    rows, cols = out.shape
    fill(panel, pieces)
    acc = before[...] + jnp.dot(gram[3][:, :rows], panel[0, :rows], preferred_element_type=F32)
    factor = 0.2 * math.sqrt(max(rows * PANEL, cols * math.prod(SIZES[n] for n in COL)))
    out[...] = (acc * factor).astype(BF16)


def newton_step(matrix):
    rows, cols = matrix.shape
    size = rows // RING
    place = jnp.stack([lax.axis_index("z"), lax.axis_index("c")]).astype(jnp.int32)
    width, _, _, height = packing(rows, cols)
    flat = array((rows + height, width))
    block = array((rows, cols))

    packed, own = call(pack_body, place, (matrix,), [flat, block], fixed=False)
    near = near_blocks(packed)
    r20 = halves_of(near[0], near[1])
    part = array((RING, size, 2 * rows))
    wide = array((4, rows, 2 * rows))
    sums = array((rows, cols), F32)
    work = 4 * rows * rows * cols

    def room(count, kind=BF16, width=cols):
        return pltpu.VMEM((count, 2 * rows, width), kind)

    pairs = pltpu.VMEM((2, rows, 2 * rows), F32)
    keep, send, low, partner = call(
        gram_body,
        place,
        (own, packed, *near),
        [part, part, array((3, 2 * rows, cols)), array((rows, 2 * rows), F32)],
        3 * work,
        [pltpu.VMEM((3, rows, 2 * rows), F32), pltpu.VMEM((2, rows, cols), BF16)],
    )
    halves = [keep, shift(send, "c", 1)]
    scratch = [pairs, room(1), pltpu.VMEM((2, rows, cols), BF16), pltpu.VMEM((2, rows, rows), F32)]
    keep, send = call(late_body, place, (own, low, partner, *r20), [part, part], work, scratch)
    halves += [keep, shift(send, "c", 1)]
    r11 = shift(near[2], "x", 1)
    r31 = shift(near[2], "x", -1)
    r21 = jnp.concatenate(r20, 0)
    r21 = shift(r21, "yl", 1)
    panel = call(panel_body, place, (low, r11, r31, r21, *r20), array((4, 2 * rows, cols)), 0, [room(2)])
    one, two = array((size, 2 * rows)), array((2 * size, 2 * rows))
    parts = call(pair_body, place, halves, [two] * FAR + [one] * 2 + [two] * (FAR - 1))
    part = {d: parts[d if d < FAR else d + 1] for d in range(RING) if d != FAR}
    mine, ahead = ring_sum(place, part, parts[FAR], parts[FAR + 1])
    across = shift(mine, "yh", 1)
    same = shift(ahead, "yl", 1)
    cross = fetch(ahead, ("yl", "yh"), lambda y, h: (y + 1, h + 1))
    mine = call(join_body, place, (mine, across, same, cross), array(mine.shape))

    ring = {0: mine}
    up, down = mine, mine
    for step in range(1, FAR):
        up = shift(up, "z", 1)
        down = shift(down, "z", -1)
        ring[step], ring[RING - step] = up, down
    ends = [shift(up[:size], "z", 1)]
    ends.append(shift(down[size:], "z", -1))
    pieces = [ring[d] for d in range(RING) if d != FAR]
    group = call(group_body, place, pieces, array((RING - 1, 2 * size, 2 * rows)))
    ends = jnp.concatenate(ends, 0)

    other = shift(group, "c", 1)
    gram, total = call(own_rows_body, place, (panel, group), [wide, sums], 2 * work)
    gram, total = call(other_rows_body, place, (panel, other, gram, total), [wide, sums], 2 * work, alias={3: 0, 4: 1})
    gram, w_high, w_low = call(
        update_body,
        place,
        (own, panel, gram, total, ends, shift(ends, "c", 1)),
        [wide, flat, block],
        work // 2,
        [pltpu.VMEM((rows, cols), F32), pltpu.VMEM((size, cols), F32)],
        alias={3: 0},
    )

    near = near_blocks(w_high)
    _, r30, r01 = near
    r20, r11, r31 = lax.optimization_barrier((shift(r30, "x", -1), shift(r01, "x", 1), shift(r30, "yl", 1)))
    blocks = (own, w_low, gram, w_high, *near, r11, r31, r20)
    total = call(near_body, place, blocks, sums, 5 * work, [room(5)])
    r21 = halves_of(r11, r31)
    return call(far_body, place, (total, gram, *r21), block, work // 2, [room(1)], home=True)


def solution(mesh):
    fine = Mesh(mesh.devices.reshape(tuple(SIZES.values())), AXES)
    return jax.shard_map(newton_step, mesh=fine, in_specs=(P(ROW, COL),), out_specs=P(ROW, COL), check_vma=False)
```

```python
import itertools
import math

import jax
import jax.numpy as jnp
from jax import lax
from jax.experimental import pallas as pl
from jax.experimental.pallas import tpu as pltpu
from jax.sharding import Mesh
from jax.sharding import PartitionSpec as P


coef_a = 3.4445
coef_b = -4.775
coef_c = 2.0315


SIZES = {"x": 4, "yl": 2, "z": 8, "yh": 2, "c": 2}
AXES = tuple(SIZES)
ROW = ("x", "yl")
COL = ("z", "yh", "c")
RING = SIZES["z"]
PANEL = SIZES["x"] * SIZES["yl"]
FAR = RING // 2
LANES = 128
VMEM_LIMIT = 14 << 20

F32 = jnp.float32
BF16 = jnp.bfloat16
VMEM = pl.BlockSpec(memory_space=pltpu.VMEM)
SMEM = pl.BlockSpec(memory_space=pltpu.SMEM)


def array(shape, kind=BF16):
    return jax.ShapeDtypeStruct(shape, kind)


def shift(value, axis, step):
    size = SIZES[axis]
    return lax.ppermute(value, axis, [((i + step) % size, i) for i in range(size)])


def fetch(value, axes, source):
    sizes = [SIZES[a] for a in axes]

    def flat(position):
        index = 0
        for p, n in zip(position, sizes, strict=True):
            index = index * n + p % n
        return index

    places = list(itertools.product(*(range(n) for n in sizes)))
    return lax.ppermute(value, axes, [(flat(source(*p)), flat(p)) for p in places])


def call(body, place, operands, outs, flops=0, scratch=(), fixed=True, home=False, alias=None):
    if fixed:
        operands = [pltpu.with_memory_space_constraint(a, pltpu.VMEM) for a in operands]
    single = not isinstance(outs, list)
    outs = [outs] if single else outs
    moved = sum(math.prod(a.shape) * 2 for a in (*operands, *outs))
    got = pl.pallas_call(
        body,
        out_shape=outs if home else [pltpu.VMEM(o.shape, o.dtype) for o in outs],
        in_specs=[SMEM] + [VMEM] * len(operands),
        out_specs=[VMEM] * len(outs),
        scratch_shapes=list(scratch),
        input_output_aliases=alias or {},
        cost_estimate=pl.CostEstimate(flops=flops, bytes_accessed=moved, transcendentals=0),
        compiler_params=pltpu.CompilerParams(vmem_limit_bytes=VMEM_LIMIT),
    )(place, *operands)
    return got[0] if single else got


def near_blocks(own):
    return lax.optimization_barrier((shift(own, "x", 1), shift(own, "x", -1), shift(own, "yl", 1)))


def halves_of(near_up, near_down):
    half = (near_up.shape[0] // 2 + 15) // 16 * 16
    first = shift(near_up[:half], "x", 1)
    return first, shift(near_down[half:], "x", -1)


def packing(rows, cols):
    width = cols // LANES * LANES
    rest = cols - width
    groups = width // rest
    return width, rest, groups, rows // groups


def pack(block, out):
    rows, cols = block.shape
    width, rest, groups, height = packing(rows, cols)
    out[:rows] = block[:, :width].astype(BF16)
    for g in range(groups):
        out[rows:, g * rest : (g + 1) * rest] = block[g * height : (g + 1) * height, width:].astype(BF16)


def copy_rows(panel, i, begin, ref, rows, width):
    step = math.gcd(math.gcd(rows, begin), 64)

    @pl.loop(0, rows // step)
    def _(k):
        at = pl.multiple_of(k * step, step)
        panel[i, pl.ds(begin + at, step), :width] = ref[pl.ds(at, step), :]


def fill(panel, refs, skip=0):
    half, cols = panel.shape[1:]
    rows = half // 2
    width, rest, groups, height = packing(rows, cols)
    total = rows + height
    at = skip * total
    for ref in refs:
        size = ref.shape[0]
        block, begin = divmod(at, total)
        i, base = divmod(block * rows, half)
        main = min(size, rows - begin)
        copy_rows(panel, i, base + begin, ref, main, width)
        if begin + size == total:
            for g in range(groups):
                low = base + g * height
                panel[i, low : low + height, width:] = ref[main:, g * rest : (g + 1) * rest]
        at += size


def pack_body(place, own, packed, copy):
    value = own[...]
    copy[...] = value
    pack(value.astype(F32), packed)


def chunk(z, far, size):
    return pl.ds(pl.multiple_of(lax.rem(z + far, RING) * size, 8), size)


DIMS = (((1,), (1,)), ((), ()))


def gram_body(place, own, *refs):
    *blocks, keep, send, panel, partner, rows, left = refs
    fill(panel, blocks)
    z, c = place[0], place[1]
    height = own.shape[0]
    panel[2, :height] = panel[0, height:]
    panel[2, height:] = panel[1, :height]
    left[0], left[1] = own[...], panel[1, height:]

    @pl.loop(0, 3)
    def _(i):
        rows[i] = lax.dot_general(left[jnp.where(i == 2, 1, 0)], panel[i], DIMS, preferred_element_type=F32)

    partner[...] = rows[2]
    split_units(z, c, rows, keep, send)


def split_units(z, c, rows, keep, send):
    size = keep.shape[1]

    @pl.loop(0, RING)
    def _(far):
        for side, out in ((c, keep), (1 - c, send)):
            out[far] = rows[side, chunk(z, far, size), :].astype(BF16)


def late_body(place, own, low, partner, top, bottom, keep, send, rows, panel, left, blocks):
    z, c = place[0], place[1]
    height = own.shape[0]
    fill(panel, [top, bottom])
    rows[0] = partner[...]
    left[0], left[1] = low[1, height:], own[...]

    @pl.loop(0, 2)
    def _(i):
        blocks[i] = lax.dot_general(left[i], panel[0, :height], DIMS, preferred_element_type=F32)

    rows[1, :, :height] = blocks[0]
    rows[1, :, height:] = blocks[1]
    split_units(z, c, rows, keep, send)


def panel_body(place, low, *refs):
    *blocks, panel, high = refs
    fill(high, blocks)

    @pl.loop(0, 2)
    def _(i):
        panel[i] = low[i]
        panel[i + 2] = high[i]


def pair_body(place, low, low_other, high, high_other, *outs):
    size = low.shape[1]
    for d in range(RING):
        lower = (low[d].astype(F32) + low_other[d].astype(F32)).astype(BF16)
        upper = (high[d].astype(F32) + high_other[d].astype(F32)).astype(BF16)
        if d == FAR:
            outs[d][...] = lower
            outs[d + 1][...] = upper
        else:
            out = outs[d if d < FAR else d + 1]
            out[:size] = lower
            out[size:] = upper


def add(a, b):
    return (a.astype(F32) + b.astype(F32)).astype(BF16)


def ring_sum(place, part, up, down):
    size = up.shape[0]
    for step in range(FAR - 1, -1, -1):
        up = shift(up, "z", -1)
        down = shift(down, "z", 1)
        if step == 0:
            return call(sum_body, place, (part[0], up, down), [array(part[0].shape), array((size, up.shape[1]))])
        elif step == FAR - 1:
            one, two = part[step], part[RING - step]
            up = jnp.concatenate([add(one[:size], up), one[size:]], 0)
            down = jnp.concatenate([two[:size], add(two[size:], down)], 0)
        else:
            up, down = add(part[step], up), add(part[RING - step], down)


def sum_body(place, near, up, down, mine, ahead):
    size = ahead.shape[0]
    total = near[...].astype(F32) + up[...].astype(F32) + down[...].astype(F32)
    mine[...] = total.astype(BF16)
    ahead[...] = total[size:].astype(BF16)


def join_body(place, mine, across, same, cross, out):
    size, width = same.shape
    own = mine[...].astype(F32) + across[...].astype(F32)
    ahead = same[...].astype(F32) + cross[...].astype(F32)
    right = lax.broadcasted_iota(jnp.int32, (size, width), 1) >= width // 2
    out[:size] = own[:size].astype(BF16)
    out[size:] = jnp.where(right & (place[1] == 1), own[size:], ahead).astype(BF16)


def group_body(place, *refs):
    *pieces, out = refs
    for i, ref in enumerate(pieces):
        out[i] = ref[...]


def lay(gram, side, group, z):
    size = gram.shape[1] // RING

    @pl.loop(0, RING - 1)
    def _(i):
        where = chunk(z, i + jnp.where(i >= FAR, 1, 0), size)
        gram[side, where, :] = group[i, :size]
        gram[side + 2, where, :] = group[i, size:]

    @pl.loop(0, 2)
    def _(i):
        gram[side + 2 * i, chunk(z, FAR, size), :] = jnp.zeros((size, gram.shape[2]), BF16)


def own_rows_body(place, panel, group, gram, total):
    z, c = place[0], place[1]
    lay(gram, c, group, z)
    total[...] = jnp.zeros(total.shape, F32)

    @pl.loop(0, 2)
    def _(i):
        total[...] += jnp.dot(gram[c + 2 * i], panel[c + 2 * i], preferred_element_type=F32)


def other_rows_body(place, panel, group, before_gram, before, gram, total):
    z, side = place[0], 1 - place[1]
    lay(gram, side, group, z)

    @pl.loop(0, 2)
    def _(i):
        total[...] += jnp.dot(gram[side + 2 * i], panel[side + 2 * i], preferred_element_type=F32)


def update_body(place, own, panel, before_gram, before, mine, other, gram, w_high, w_low, total, acc):
    z, c = place[0], place[1]
    size = gram.shape[1] // RING
    where = chunk(z, FAR, size)
    for side, ref in ((c, mine), (1 - c, other)):
        gram[side, where, :] = ref[:size]
        gram[side + 2, where, :] = ref[size:]
    acc[...] = jnp.zeros(acc.shape, F32)

    @pl.loop(0, 4)
    def _(i):
        acc[...] += jnp.dot(gram[i, where, :], panel[i], preferred_element_type=F32)

    total[...] = before[...]
    total[where, :] = acc[...]
    w = coef_b * own[...].astype(F32) + coef_c * total[...]
    pack(w, w_high)
    w_low[...] = (w - w.astype(BF16).astype(F32)).astype(BF16)


def near_body(place, own, w_low, gram, *refs):
    *blocks, total, panel = refs
    rows = own.shape[0]
    fill(panel, blocks)
    panel[2, :rows] = w_low[...]
    panel[2, rows:] = jnp.zeros((rows, own.shape[1]), BF16)
    total[...] = coef_a * own[...].astype(F32)

    @pl.loop(0, 3)
    def _(i):
        total[...] += jnp.dot(gram[jnp.where(i == 2, 0, i)], panel[i], preferred_element_type=F32)


def side_body(place, before, gram, r11, r31, r20, total, panel):
    rows = total.shape[0]
    fill(panel, [r11, r31])
    fill(panel, [r20], 3)
    panel[1, :rows] = jnp.zeros((rows, total.shape[1]), BF16)
    total[...] = before[...]

    @pl.loop(0, 2)
    def _(i):
        total[...] += jnp.dot(gram[i + 2], panel[i], preferred_element_type=F32)


def far_body(place, before, gram, *refs):
    *pieces, out, panel = refs
    rows, cols = out.shape
    fill(panel, pieces)
    acc = before[...] + jnp.dot(gram[3][:, :rows], panel[0, :rows], preferred_element_type=F32)
    factor = 0.2 * math.sqrt(max(rows * PANEL, cols * math.prod(SIZES[n] for n in COL)))
    out[...] = (acc * factor).astype(BF16)


def newton_step(matrix):
    rows, cols = matrix.shape
    size = rows // RING
    place = jnp.stack([lax.axis_index("z"), lax.axis_index("c")]).astype(jnp.int32)
    width, _, _, height = packing(rows, cols)
    flat = array((rows + height, width))
    block = array((rows, cols))

    packed, own = call(pack_body, place, (matrix,), [flat, block], fixed=False)
    near = near_blocks(packed)
    r20 = halves_of(near[0], near[1])
    part = array((RING, size, 2 * rows))
    wide = array((4, rows, 2 * rows))
    sums = array((rows, cols), F32)
    work = 4 * rows * rows * cols

    def room(count, kind=BF16, width=cols):
        return pltpu.VMEM((count, 2 * rows, width), kind)

    pairs = pltpu.VMEM((2, rows, 2 * rows), F32)
    keep, send, low, partner = call(
        gram_body,
        place,
        (own, packed, *near),
        [part, part, array((3, 2 * rows, cols)), array((rows, 2 * rows), F32)],
        3 * work,
        [pltpu.VMEM((3, rows, 2 * rows), F32), pltpu.VMEM((2, rows, cols), BF16)],
    )
    halves = [keep, shift(send, "c", 1)]
    scratch = [pairs, room(1), pltpu.VMEM((2, rows, cols), BF16), pltpu.VMEM((2, rows, rows), F32)]
    keep, send = call(late_body, place, (own, low, partner, *r20), [part, part], work, scratch)
    halves += [keep, shift(send, "c", 1)]
    r11 = shift(near[2], "x", 1)
    r31 = shift(near[2], "x", -1)
    r21 = jnp.concatenate(r20, 0)
    r21 = shift(r21, "yl", 1)
    panel = call(panel_body, place, (low, r11, r31, r21, *r20), array((4, 2 * rows, cols)), 0, [room(2)])
    one, two = array((size, 2 * rows)), array((2 * size, 2 * rows))
    parts = call(pair_body, place, halves, [two] * FAR + [one] * 2 + [two] * (FAR - 1))
    part = {d: parts[d if d < FAR else d + 1] for d in range(RING) if d != FAR}
    mine, ahead = ring_sum(place, part, parts[FAR], parts[FAR + 1])
    across = shift(mine, "yh", 1)
    same = shift(ahead, "yl", 1)
    cross = fetch(ahead, ("yl", "yh"), lambda y, h: (y + 1, h + 1))
    mine = call(join_body, place, (mine, across, same, cross), array(mine.shape))

    ring = {0: mine}
    up, down = mine, mine
    for step in range(1, FAR):
        up = shift(up, "z", 1)
        down = shift(down, "z", -1)
        ring[step], ring[RING - step] = up, down
    ends = [shift(up[:size], "z", 1)]
    ends.append(shift(down[size:], "z", -1))
    pieces = [ring[d] for d in range(RING) if d != FAR]
    group = call(group_body, place, pieces, array((RING - 1, 2 * size, 2 * rows)))
    ends = jnp.concatenate(ends, 0)

    other = shift(group, "c", 1)
    gram, total = call(own_rows_body, place, (panel, group), [wide, sums], 2 * work)
    gram, total = call(other_rows_body, place, (panel, other, gram, total), [wide, sums], 2 * work, alias={3: 0, 4: 1})
    gram, w_high, w_low = call(
        update_body,
        place,
        (own, panel, gram, total, ends, shift(ends, "c", 1)),
        [wide, flat, block],
        work // 2,
        [pltpu.VMEM((rows, cols), F32), pltpu.VMEM((size, cols), F32)],
        alias={3: 0},
    )

    near = near_blocks(w_high)
    _, r30, r01 = near
    r20 = shift(r30, "x", -1)
    r11 = shift(r01, "x", 1)
    r31 = shift(r30, "yl", 1)
    r20, r11, r31 = lax.optimization_barrier((r20, r11, r31))
    total = call(near_body, place, (own, w_low, gram, w_high, *near), sums, 3 * work, [room(3)])
    total = call(side_body, place, (total, gram, r11, r31, r20), sums, 2 * work, [room(2)])
    r21 = halves_of(r11, r31)
    return call(far_body, place, (total, gram, *r21), block, work // 2, [room(1)], home=True)


def solution(mesh):
    fine = Mesh(mesh.devices.reshape(tuple(SIZES.values())), AXES)
    return jax.shard_map(newton_step, mesh=fine, in_specs=(P(ROW, COL),), out_specs=P(ROW, COL), check_vma=False)
```

```python
import itertools
import math

import jax
import jax.numpy as jnp
from jax import lax
from jax.experimental import pallas as pl
from jax.experimental.pallas import tpu as pltpu
from jax.sharding import Mesh
from jax.sharding import PartitionSpec as P


coef_a = 3.4445
coef_b = -4.775
coef_c = 2.0315


SIZES = {"x": 4, "yl": 2, "z": 8, "yh": 2, "c": 2}
AXES = tuple(SIZES)
ROW = ("x", "yl")
COL = ("z", "yh", "c")
RING = SIZES["z"]
PANEL = SIZES["x"] * SIZES["yl"]
FAR = RING // 2
LANES = 128
VMEM_LIMIT = 14 << 20

F32 = jnp.float32
BF16 = jnp.bfloat16
VMEM = pl.BlockSpec(memory_space=pltpu.VMEM)
SMEM = pl.BlockSpec(memory_space=pltpu.SMEM)


def array(shape, kind=BF16):
    return jax.ShapeDtypeStruct(shape, kind)


def shift(value, axis, step):
    size = SIZES[axis]
    return lax.ppermute(value, axis, [((i + step) % size, i) for i in range(size)])


def fetch(value, axes, source):
    sizes = [SIZES[a] for a in axes]

    def flat(position):
        index = 0
        for p, n in zip(position, sizes, strict=True):
            index = index * n + p % n
        return index

    places = list(itertools.product(*(range(n) for n in sizes)))
    return lax.ppermute(value, axes, [(flat(source(*p)), flat(p)) for p in places])


def call(body, place, operands, outs, flops=0, scratch=(), fixed=True, home=False, alias=None):
    if fixed:
        operands = [pltpu.with_memory_space_constraint(a, pltpu.VMEM) for a in operands]
    single = not isinstance(outs, list)
    outs = [outs] if single else outs
    moved = sum(math.prod(a.shape) * 2 for a in (*operands, *outs))
    got = pl.pallas_call(
        body,
        out_shape=outs if home else [pltpu.VMEM(o.shape, o.dtype) for o in outs],
        in_specs=[SMEM] + [VMEM] * len(operands),
        out_specs=[VMEM] * len(outs),
        scratch_shapes=list(scratch),
        input_output_aliases=alias or {},
        cost_estimate=pl.CostEstimate(flops=flops, bytes_accessed=moved, transcendentals=0),
        compiler_params=pltpu.CompilerParams(vmem_limit_bytes=VMEM_LIMIT),
    )(place, *operands)
    return got[0] if single else got


def near_blocks(own):
    return lax.optimization_barrier((shift(own, "x", 1), shift(own, "x", -1), shift(own, "yl", 1)))


def halves_of(near_up, near_down):
    half = (near_up.shape[0] // 2 + 15) // 16 * 16
    first = shift(near_up[:half], "x", 1)
    return first, shift(near_down[half:], "x", -1)


def packing(rows, cols):
    width = cols // LANES * LANES
    rest = cols - width
    groups = width // rest
    return width, rest, groups, rows // groups


def pack(block, out):
    rows, cols = block.shape
    width, rest, groups, height = packing(rows, cols)
    out[:rows] = block[:, :width].astype(BF16)
    for g in range(groups):
        out[rows:, g * rest : (g + 1) * rest] = block[g * height : (g + 1) * height, width:].astype(BF16)


def copy_rows(panel, i, begin, ref, rows, width):
    step = math.gcd(math.gcd(rows, begin), 64)

    @pl.loop(0, rows // step)
    def _(k):
        at = pl.multiple_of(k * step, step)
        panel[i, pl.ds(begin + at, step), :width] = ref[pl.ds(at, step), :]


def fill(panel, refs, skip=0):
    half, cols = panel.shape[1:]
    rows = half // 2
    width, rest, groups, height = packing(rows, cols)
    total = rows + height
    at = skip * total
    for ref in refs:
        size = ref.shape[0]
        block, begin = divmod(at, total)
        i, base = divmod(block * rows, half)
        main = min(size, rows - begin)
        copy_rows(panel, i, base + begin, ref, main, width)
        if begin + size == total:
            for g in range(groups):
                low = base + g * height
                panel[i, low : low + height, width:] = ref[main:, g * rest : (g + 1) * rest]
        at += size


def pack_body(place, own, packed, copy):
    value = own[...]
    copy[...] = value
    pack(value.astype(F32), packed)


def chunk(z, far, size):
    return pl.ds(pl.multiple_of(lax.rem(z + far, RING) * size, 8), size)


DIMS = (((1,), (1,)), ((), ()))


def gram_body(place, own, *refs):
    *blocks, keep, send, panel, partner, rows, left = refs
    fill(panel, blocks)
    z, c = place[0], place[1]
    height = own.shape[0]
    panel[2, :height] = panel[0, height:]
    panel[2, height:] = panel[1, :height]
    left[0], left[1] = own[...], panel[1, height:]

    @pl.loop(0, 3)
    def _(i):
        rows[i] = lax.dot_general(left[jnp.where(i == 2, 1, 0)], panel[i], DIMS, preferred_element_type=F32)

    partner[...] = rows[2]
    split_units(z, c, rows, keep, send)


def split_units(z, c, rows, keep, send):
    size = keep.shape[1]

    @pl.loop(0, RING)
    def _(far):
        for side, out in ((c, keep), (1 - c, send)):
            out[far] = rows[side, chunk(z, far, size), :].astype(BF16)


def late_body(place, own, low, partner, top, bottom, keep, send, rows, panel, left, blocks):
    z, c = place[0], place[1]
    height = own.shape[0]
    fill(panel, [top, bottom])
    rows[0] = partner[...]
    left[0], left[1] = low[1, height:], own[...]

    @pl.loop(0, 2)
    def _(i):
        blocks[i] = lax.dot_general(left[i], panel[0, :height], DIMS, preferred_element_type=F32)

    rows[1, :, :height] = blocks[0]
    rows[1, :, height:] = blocks[1]
    split_units(z, c, rows, keep, send)


def panel_body(place, low, *refs):
    *blocks, panel, high = refs
    fill(high, blocks)

    @pl.loop(0, 2)
    def _(i):
        panel[i] = low[i]
        panel[i + 2] = high[i]


def pair_body(place, low, low_other, high, high_other, *outs):
    size = low.shape[1]
    for d, out in enumerate(outs):
        out[:size] = (low[d].astype(F32) + low_other[d].astype(F32)).astype(BF16)
        out[size:] = (high[d].astype(F32) + high_other[d].astype(F32)).astype(BF16)


def add(a, b):
    return (a.astype(F32) + b.astype(F32)).astype(BF16)


def ring_sum(place, part):
    up, down = part[FAR - 1], part[FAR + 1]
    far = shift(part[FAR], "z", FAR)
    for step in range(FAR - 2, -1, -1):
        up = shift(up, "z", -1)
        down = shift(down, "z", 1)
        if step > 0:
            up, down = add(part[step], up), add(part[RING - step], down)
    size, width = up.shape[0] // 2, up.shape[1]
    return call(sum_body, place, (part[0], up, down, far), [array(up.shape), array((size, width))])


def sum_body(place, near, up, down, far, mine, ahead):
    size = ahead.shape[0]
    total = near[...].astype(F32) + up[...].astype(F32) + down[...].astype(F32) + far[...].astype(F32)
    mine[...] = total.astype(BF16)
    ahead[...] = total[size:].astype(BF16)


def join_body(place, mine, across, same, cross, out):
    size, width = same.shape
    own = mine[...].astype(F32) + across[...].astype(F32)
    ahead = same[...].astype(F32) + cross[...].astype(F32)
    right = lax.broadcasted_iota(jnp.int32, (size, width), 1) >= width // 2
    out[:size] = own[:size].astype(BF16)
    out[size:] = jnp.where(right & (place[1] == 1), own[size:], ahead).astype(BF16)


def group_body(place, *refs):
    *pieces, out = refs
    for i, ref in enumerate(pieces):
        out[i] = ref[...]


def lay(gram, side, group, z):
    size = gram.shape[1] // RING

    @pl.loop(0, RING)
    def _(i):
        where = chunk(z, i, size)
        gram[side, where, :] = group[i, :size]
        gram[side + 2, where, :] = group[i, size:]


def own_rows_body(place, panel, group, gram, total):
    z, c = place[0], place[1]
    lay(gram, c, group, z)
    total[...] = jnp.zeros(total.shape, F32)

    @pl.loop(0, 2)
    def _(i):
        total[...] += jnp.dot(gram[c + 2 * i], panel[c + 2 * i], preferred_element_type=F32)


def other_rows_body(place, own, panel, group, before_gram, before, gram, w_high, w_low, total):
    z, side = place[0], 1 - place[1]
    lay(gram, side, group, z)
    total[...] = before[...]

    @pl.loop(0, 2)
    def _(i):
        total[...] += jnp.dot(gram[side + 2 * i], panel[side + 2 * i], preferred_element_type=F32)

    w = coef_b * own[...].astype(F32) + coef_c * total[...]
    pack(w, w_high)
    w_low[...] = (w - w.astype(BF16).astype(F32)).astype(BF16)


def near_body(place, own, w_low, gram, *refs):
    *blocks, total, panel = refs
    rows = own.shape[0]
    fill(panel, blocks)
    panel[2, :rows] = w_low[...]
    panel[2, rows:] = jnp.zeros((rows, own.shape[1]), BF16)
    total[...] = coef_a * own[...].astype(F32)

    @pl.loop(0, 3)
    def _(i):
        total[...] += jnp.dot(gram[jnp.where(i == 2, 0, i)], panel[i], preferred_element_type=F32)


def side_body(place, before, gram, r11, r31, r20, total, panel):
    rows = total.shape[0]
    fill(panel, [r11, r31])
    fill(panel, [r20], 3)
    panel[1, :rows] = jnp.zeros((rows, total.shape[1]), BF16)
    total[...] = before[...]

    @pl.loop(0, 2)
    def _(i):
        total[...] += jnp.dot(gram[i + 2], panel[i], preferred_element_type=F32)


def far_body(place, before, gram, *refs):
    *pieces, out, panel = refs
    rows, cols = out.shape
    fill(panel, pieces)
    acc = before[...] + jnp.dot(gram[3][:, :rows], panel[0, :rows], preferred_element_type=F32)
    factor = 0.2 * math.sqrt(max(rows * PANEL, cols * math.prod(SIZES[n] for n in COL)))
    out[...] = (acc * factor).astype(BF16)


def newton_step(matrix):
    rows, cols = matrix.shape
    size = rows // RING
    place = jnp.stack([lax.axis_index("z"), lax.axis_index("c")]).astype(jnp.int32)
    width, _, _, height = packing(rows, cols)
    flat = array((rows + height, width))
    block = array((rows, cols))

    packed, own = call(pack_body, place, (matrix,), [flat, block], fixed=False)
    near = near_blocks(packed)
    r20 = halves_of(near[0], near[1])
    part = array((RING, size, 2 * rows))
    wide = array((4, rows, 2 * rows))
    sums = array((rows, cols), F32)
    work = 4 * rows * rows * cols

    def room(count, kind=BF16, width=cols):
        return pltpu.VMEM((count, 2 * rows, width), kind)

    pairs = pltpu.VMEM((2, rows, 2 * rows), F32)
    keep, send, low, partner = call(
        gram_body,
        place,
        (own, packed, *near),
        [part, part, array((3, 2 * rows, cols)), array((rows, 2 * rows), F32)],
        3 * work,
        [pltpu.VMEM((3, rows, 2 * rows), F32), pltpu.VMEM((2, rows, cols), BF16)],
    )
    halves = [keep, shift(send, "c", 1)]
    scratch = [pairs, room(1), pltpu.VMEM((2, rows, cols), BF16), pltpu.VMEM((2, rows, rows), F32)]
    keep, send = call(late_body, place, (own, low, partner, *r20), [part, part], work, scratch)
    halves += [keep, shift(send, "c", 1)]
    r11 = shift(near[2], "x", 1)
    r31 = shift(near[2], "x", -1)
    r21 = jnp.concatenate(r20, 0)
    r21 = shift(r21, "yl", 1)
    panel = call(panel_body, place, (low, r11, r31, r21, *r20), array((4, 2 * rows, cols)), 0, [room(2)])
    two = array((2 * size, 2 * rows))
    parts = call(pair_body, place, halves, [two] * RING)
    mine, ahead = ring_sum(place, parts)
    across = shift(mine, "yh", 1)
    same = shift(ahead, "yl", 1)
    cross = fetch(ahead, ("yl", "yh"), lambda y, h: (y + 1, h + 1))
    mine = call(join_body, place, (mine, across, same, cross), array(mine.shape))

    ring = {0: mine}
    ring[FAR] = shift(mine, "z", FAR)
    up, down = mine, mine
    for step in range(1, FAR):
        up = shift(up, "z", 1)
        down = shift(down, "z", -1)
        ring[step], ring[RING - step] = up, down
    group = call(group_body, place, [ring[d] for d in range(RING)], array((RING, 2 * size, 2 * rows)))
    other = shift(group, "c", 1)
    gram, total = call(own_rows_body, place, (panel, group), [wide, sums], 2 * work)
    gram, w_high, w_low = call(
        other_rows_body,
        place,
        (own, panel, other, gram, total),
        [wide, flat, block],
        2 * work,
        [pltpu.VMEM((rows, cols), F32)],
        alias={4: 0},
    )

    near = near_blocks(w_high)
    _, r30, r01 = near
    r20 = shift(r30, "x", -1)
    r11 = shift(r01, "x", 1)
    r31 = shift(r30, "yl", 1)
    r20, r11, r31 = lax.optimization_barrier((r20, r11, r31))
    total = call(near_body, place, (own, w_low, gram, w_high, *near), sums, 3 * work, [room(3)])
    total = call(side_body, place, (total, gram, r11, r31, r20), sums, 2 * work, [room(2)])
    r21 = halves_of(r11, r31)
    return call(far_body, place, (total, gram, *r21), block, work // 2, [room(1)], home=True)


def solution(mesh):
    fine = Mesh(mesh.devices.reshape(tuple(SIZES.values())), AXES)
    return jax.shard_map(newton_step, mesh=fine, in_specs=(P(ROW, COL),), out_specs=P(ROW, COL), check_vma=False)
```

```python
import itertools
import math

import jax
import jax.numpy as jnp
from jax import lax
from jax.experimental import pallas as pl
from jax.experimental.pallas import tpu as pltpu
from jax.sharding import Mesh
from jax.sharding import PartitionSpec as P


coef_a = 3.4445
coef_b = -4.775
coef_c = 2.0315


SIZES = {"x": 4, "yl": 2, "z": 8, "yh": 2, "c": 2}
AXES = tuple(SIZES)
ROW = ("x", "yl")
COL = ("z", "yh", "c")
RING = SIZES["z"]
PANEL = SIZES["x"] * SIZES["yl"]
FAR = RING // 2
LANES = 128
VMEM_LIMIT = 14 << 20

F32 = jnp.float32
BF16 = jnp.bfloat16
VMEM = pl.BlockSpec(memory_space=pltpu.VMEM)
SMEM = pl.BlockSpec(memory_space=pltpu.SMEM)


def array(shape, kind=BF16):
    return jax.ShapeDtypeStruct(shape, kind)


def shift(value, axis, step):
    size = SIZES[axis]
    return lax.ppermute(value, axis, [((i + step) % size, i) for i in range(size)])


def fetch(value, axes, source):
    sizes = [SIZES[a] for a in axes]

    def flat(position):
        index = 0
        for p, n in zip(position, sizes, strict=True):
            index = index * n + p % n
        return index

    places = list(itertools.product(*(range(n) for n in sizes)))
    return lax.ppermute(value, axes, [(flat(source(*p)), flat(p)) for p in places])


def call(body, place, operands, outs, flops=0, scratch=(), fixed=True, home=False, alias=None):
    if fixed:
        operands = [pltpu.with_memory_space_constraint(a, pltpu.VMEM) for a in operands]
    single = not isinstance(outs, list)
    outs = [outs] if single else outs
    moved = sum(math.prod(a.shape) * 2 for a in (*operands, *outs))
    got = pl.pallas_call(
        body,
        out_shape=outs if home else [pltpu.VMEM(o.shape, o.dtype) for o in outs],
        in_specs=[SMEM] + [VMEM] * len(operands),
        out_specs=[VMEM] * len(outs),
        scratch_shapes=list(scratch),
        input_output_aliases=alias or {},
        cost_estimate=pl.CostEstimate(flops=flops, bytes_accessed=moved, transcendentals=0),
        compiler_params=pltpu.CompilerParams(vmem_limit_bytes=VMEM_LIMIT),
    )(place, *operands)
    return got[0] if single else got


def near_blocks(own):
    return lax.optimization_barrier((shift(own, "x", 1), shift(own, "x", -1), shift(own, "yl", 1)))


def halves_of(near_up, near_down):
    half = (near_up.shape[0] // 2 + 15) // 16 * 16
    first = shift(near_up[:half], "x", 1)
    return first, shift(near_down[half:], "x", -1)


def packing(rows, cols):
    width = cols // LANES * LANES
    rest = cols - width
    groups = width // rest
    return width, rest, groups, rows // groups


def pack(block, out):
    rows, cols = block.shape
    width, rest, groups, height = packing(rows, cols)
    out[:rows] = block[:, :width].astype(BF16)
    for g in range(groups):
        out[rows:, g * rest : (g + 1) * rest] = block[g * height : (g + 1) * height, width:].astype(BF16)


def copy_rows(panel, i, begin, ref, rows, width):
    step = math.gcd(math.gcd(rows, begin), 64)

    @pl.loop(0, rows // step)
    def _(k):
        at = pl.multiple_of(k * step, step)
        panel[i, pl.ds(begin + at, step), :width] = ref[pl.ds(at, step), :]


def fill(panel, refs, skip=0):
    half, cols = panel.shape[1:]
    rows = half // 2
    width, rest, groups, height = packing(rows, cols)
    total = rows + height
    at = skip * total
    for ref in refs:
        size = ref.shape[0]
        block, begin = divmod(at, total)
        i, base = divmod(block * rows, half)
        main = min(size, rows - begin)
        copy_rows(panel, i, base + begin, ref, main, width)
        if begin + size == total:
            for g in range(groups):
                low = base + g * height
                panel[i, low : low + height, width:] = ref[main:, g * rest : (g + 1) * rest]
        at += size


def pack_body(place, own, packed, copy):
    value = own[...]
    copy[...] = value
    pack(value.astype(F32), packed)


def chunk(z, far, size):
    return pl.ds(pl.multiple_of(lax.rem(z + far, RING) * size, 8), size)


DIMS = (((1,), (1,)), ((), ()))


def gram_body(place, own, *refs):
    *blocks, keep, send, panel, partner, rows, left = refs
    fill(panel, blocks)
    z, c = place[0], place[1]
    height = own.shape[0]
    panel[2, :height] = panel[0, height:]
    panel[2, height:] = panel[1, :height]
    left[0], left[1] = own[...], panel[1, height:]

    @pl.loop(0, 3)
    def _(i):
        rows[i] = lax.dot_general(left[jnp.where(i == 2, 1, 0)], panel[i], DIMS, preferred_element_type=F32)

    partner[...] = rows[2]
    split_units(z, c, rows, keep, send)


def split_units(z, c, rows, keep, send):
    size = keep.shape[1]

    @pl.loop(0, RING)
    def _(far):
        for side, out in ((c, keep), (1 - c, send)):
            out[far] = rows[side, chunk(z, far, size), :].astype(BF16)


def late_body(place, own, low, partner, top, bottom, keep, send, rows, panel, left, blocks):
    z, c = place[0], place[1]
    height = own.shape[0]
    fill(panel, [top, bottom])
    rows[0] = partner[...]
    left[0], left[1] = low[1, height:], own[...]

    @pl.loop(0, 2)
    def _(i):
        blocks[i] = lax.dot_general(left[i], panel[0, :height], DIMS, preferred_element_type=F32)

    rows[1, :, :height] = blocks[0]
    rows[1, :, height:] = blocks[1]
    split_units(z, c, rows, keep, send)


def panel_body(place, low, *refs):
    *blocks, panel, high = refs
    fill(high, blocks)

    @pl.loop(0, 2)
    def _(i):
        panel[i] = low[i]
        panel[i + 2] = high[i]


def pair_body(place, low, low_other, high, high_other, *outs):
    size = low.shape[1]
    for d in range(RING):
        lower = (low[d].astype(F32) + low_other[d].astype(F32)).astype(BF16)
        upper = (high[d].astype(F32) + high_other[d].astype(F32)).astype(BF16)
        if d == FAR:
            outs[d][...] = lower
            outs[d + 1][...] = upper
        else:
            out = outs[d if d < FAR else d + 1]
            out[:size] = lower
            out[size:] = upper


def add(a, b):
    return (a.astype(F32) + b.astype(F32)).astype(BF16)


def ring_sum(place, part, up, down):
    size = up.shape[0]
    for step in range(FAR - 1, -1, -1):
        up = shift(up, "z", -1)
        down = shift(down, "z", 1)
        if step == 0:
            return call(sum_body, place, (part[0], up, down), [array(part[0].shape), array((size, up.shape[1]))])
        elif step == FAR - 1:
            one, two = part[step], part[RING - step]
            up = jnp.concatenate([add(one[:size], up), one[size:]], 0)
            down = jnp.concatenate([two[:size], add(two[size:], down)], 0)
        else:
            up, down = add(part[step], up), add(part[RING - step], down)


def sum_body(place, near, up, down, mine, ahead):
    size = ahead.shape[0]
    total = near[...].astype(F32) + up[...].astype(F32) + down[...].astype(F32)
    mine[...] = total.astype(BF16)
    ahead[...] = total[size:].astype(BF16)


def join_body(place, mine, across, same, cross, out):
    size, width = same.shape
    own = mine[...].astype(F32) + across[...].astype(F32)
    ahead = same[...].astype(F32) + cross[...].astype(F32)
    right = lax.broadcasted_iota(jnp.int32, (size, width), 1) >= width // 2
    out[:size] = own[:size].astype(BF16)
    out[size:] = jnp.where(right & (place[1] == 1), own[size:], ahead).astype(BF16)


def group_body(place, *refs):
    *pieces, out = refs
    for i, ref in enumerate(pieces):
        out[i] = ref[...]


def lay(gram, side, group, z):
    size = gram.shape[1] // RING

    @pl.loop(0, RING)
    def _(i):
        where = chunk(z, i, size)
        gram[side, where, :] = group[i, :size]
        gram[side + 2, where, :] = group[i, size:]


def own_rows_body(place, panel, group, gram, total):
    z, c = place[0], place[1]
    lay(gram, c, group, z)
    total[...] = jnp.zeros(total.shape, F32)

    @pl.loop(0, 2)
    def _(i):
        total[...] += jnp.dot(gram[c + 2 * i], panel[c + 2 * i], preferred_element_type=F32)


def other_rows_body(place, own, panel, group, before_gram, before, gram, w_high, w_low, total):
    z, side = place[0], 1 - place[1]
    lay(gram, side, group, z)
    total[...] = before[...]

    @pl.loop(0, 2)
    def _(i):
        total[...] += jnp.dot(gram[side + 2 * i], panel[side + 2 * i], preferred_element_type=F32)

    w = coef_b * own[...].astype(F32) + coef_c * total[...]
    pack(w, w_high)
    w_low[...] = (w - w.astype(BF16).astype(F32)).astype(BF16)


def near_body(place, own, w_low, gram, *refs):
    *blocks, total, panel = refs
    rows = own.shape[0]
    fill(panel, blocks)
    panel[2, :rows] = w_low[...]
    panel[2, rows:] = jnp.zeros((rows, own.shape[1]), BF16)
    total[...] = coef_a * own[...].astype(F32)

    @pl.loop(0, 3)
    def _(i):
        total[...] += jnp.dot(gram[jnp.where(i == 2, 0, i)], panel[i], preferred_element_type=F32)


def side_body(place, before, gram, r11, r31, r20, total, panel):
    rows = total.shape[0]
    fill(panel, [r11, r31])
    fill(panel, [r20], 3)
    panel[1, :rows] = jnp.zeros((rows, total.shape[1]), BF16)
    total[...] = before[...]

    @pl.loop(0, 2)
    def _(i):
        total[...] += jnp.dot(gram[i + 2], panel[i], preferred_element_type=F32)


def far_body(place, before, gram, *refs):
    *pieces, out, panel = refs
    rows, cols = out.shape
    fill(panel, pieces)
    acc = before[...] + jnp.dot(gram[3][:, :rows], panel[0, :rows], preferred_element_type=F32)
    factor = 0.2 * math.sqrt(max(rows * PANEL, cols * math.prod(SIZES[n] for n in COL)))
    out[...] = (acc * factor).astype(BF16)


def newton_step(matrix):
    rows, cols = matrix.shape
    size = rows // RING
    place = jnp.stack([lax.axis_index("z"), lax.axis_index("c")]).astype(jnp.int32)
    width, _, _, height = packing(rows, cols)
    flat = array((rows + height, width))
    block = array((rows, cols))

    packed, own = call(pack_body, place, (matrix,), [flat, block], fixed=False)
    near = near_blocks(packed)
    r20 = halves_of(near[0], near[1])
    part = array((RING, size, 2 * rows))
    wide = array((4, rows, 2 * rows))
    sums = array((rows, cols), F32)
    work = 4 * rows * rows * cols

    def room(count, kind=BF16, width=cols):
        return pltpu.VMEM((count, 2 * rows, width), kind)

    pairs = pltpu.VMEM((2, rows, 2 * rows), F32)
    keep, send, low, partner = call(
        gram_body,
        place,
        (own, packed, *near),
        [part, part, array((3, 2 * rows, cols)), array((rows, 2 * rows), F32)],
        3 * work,
        [pltpu.VMEM((3, rows, 2 * rows), F32), pltpu.VMEM((2, rows, cols), BF16)],
    )
    halves = [keep, shift(send, "c", 1)]
    scratch = [pairs, room(1), pltpu.VMEM((2, rows, cols), BF16), pltpu.VMEM((2, rows, rows), F32)]
    keep, send = call(late_body, place, (own, low, partner, *r20), [part, part], work, scratch)
    halves += [keep, shift(send, "c", 1)]
    r11 = shift(near[2], "x", 1)
    r31 = shift(near[2], "x", -1)
    r21 = jnp.concatenate(r20, 0)
    r21 = shift(r21, "yl", 1)
    panel = call(panel_body, place, (low, r11, r31, r21, *r20), array((4, 2 * rows, cols)), 0, [room(2)])
    one, two = array((size, 2 * rows)), array((2 * size, 2 * rows))
    parts = call(pair_body, place, halves, [two] * FAR + [one] * 2 + [two] * (FAR - 1))
    part = {d: parts[d if d < FAR else d + 1] for d in range(RING) if d != FAR}
    mine, ahead = ring_sum(place, part, parts[FAR], parts[FAR + 1])
    across = shift(mine, "yh", 1)
    same = shift(ahead, "yl", 1)
    cross = fetch(ahead, ("yl", "yh"), lambda y, h: (y + 1, h + 1))
    mine = call(join_body, place, (mine, across, same, cross), array(mine.shape))

    ring = {0: mine}
    ring[FAR] = shift(mine, "z", FAR)
    up, down = mine, mine
    for step in range(1, FAR):
        up = shift(up, "z", 1)
        down = shift(down, "z", -1)
        ring[step], ring[RING - step] = up, down
    group = call(group_body, place, [ring[d] for d in range(RING)], array((RING, 2 * size, 2 * rows)))
    other = shift(group, "c", 1)
    gram, total = call(own_rows_body, place, (panel, group), [wide, sums], 2 * work)
    gram, w_high, w_low = call(
        other_rows_body,
        place,
        (own, panel, other, gram, total),
        [wide, flat, block],
        2 * work,
        [pltpu.VMEM((rows, cols), F32)],
        alias={4: 0},
    )

    near = near_blocks(w_high)
    _, r30, r01 = near
    r20 = shift(r30, "x", -1)
    r11 = shift(r01, "x", 1)
    r31 = shift(r30, "yl", 1)
    r20, r11, r31 = lax.optimization_barrier((r20, r11, r31))
    total = call(near_body, place, (own, w_low, gram, w_high, *near), sums, 3 * work, [room(3)])
    total = call(side_body, place, (total, gram, r11, r31, r20), sums, 2 * work, [room(2)])
    r21 = halves_of(r11, r31)
    return call(far_body, place, (total, gram, *r21), block, work // 2, [room(1)], home=True)


def solution(mesh):
    fine = Mesh(mesh.devices.reshape(tuple(SIZES.values())), AXES)
    return jax.shard_map(newton_step, mesh=fine, in_specs=(P(ROW, COL),), out_specs=P(ROW, COL), check_vma=False)
```

```python
import itertools
import math

import jax
import jax.numpy as jnp
from jax import lax
from jax.experimental import pallas as pl
from jax.experimental.pallas import tpu as pltpu
from jax.sharding import Mesh
from jax.sharding import PartitionSpec as P


coef_a = 3.4445
coef_b = -4.775
coef_c = 2.0315


SIZES = {"x": 4, "yl": 2, "z": 8, "yh": 2, "c": 2}
AXES = tuple(SIZES)
ROW = ("x", "yl")
COL = ("z", "yh", "c")
RING = SIZES["z"]
PANEL = SIZES["x"] * SIZES["yl"]
FAR = RING // 2
LANES = 128
VMEM_LIMIT = 14 << 20

F32 = jnp.float32
BF16 = jnp.bfloat16
VMEM = pl.BlockSpec(memory_space=pltpu.VMEM)
SMEM = pl.BlockSpec(memory_space=pltpu.SMEM)


def array(shape, kind=BF16):
    return jax.ShapeDtypeStruct(shape, kind)


def shift(value, axis, step):
    size = SIZES[axis]
    return lax.ppermute(value, axis, [((i + step) % size, i) for i in range(size)])


def fetch(value, axes, source):
    sizes = [SIZES[a] for a in axes]

    def flat(position):
        index = 0
        for p, n in zip(position, sizes, strict=True):
            index = index * n + p % n
        return index

    places = list(itertools.product(*(range(n) for n in sizes)))
    return lax.ppermute(value, axes, [(flat(source(*p)), flat(p)) for p in places])


def call(body, place, operands, outs, flops=0, scratch=(), fixed=True, home=False, alias=None):
    if fixed:
        operands = [pltpu.with_memory_space_constraint(a, pltpu.VMEM) for a in operands]
    single = not isinstance(outs, list)
    outs = [outs] if single else outs
    moved = sum(math.prod(a.shape) * 2 for a in (*operands, *outs))
    got = pl.pallas_call(
        body,
        out_shape=outs if home else [pltpu.VMEM(o.shape, o.dtype) for o in outs],
        in_specs=[SMEM] + [VMEM] * len(operands),
        out_specs=[VMEM] * len(outs),
        scratch_shapes=list(scratch),
        input_output_aliases=alias or {},
        cost_estimate=pl.CostEstimate(flops=flops, bytes_accessed=moved, transcendentals=0),
        compiler_params=pltpu.CompilerParams(vmem_limit_bytes=VMEM_LIMIT),
    )(place, *operands)
    return got[0] if single else got


def near_blocks(own):
    return lax.optimization_barrier((shift(own, "x", 1), shift(own, "x", -1), shift(own, "yl", 1)))


def halves_of(near_up, near_down):
    half = (near_up.shape[0] // 2 + 15) // 16 * 16
    first = shift(near_up[:half], "x", 1)
    return first, shift(near_down[half:], "x", -1)


def packing(rows, cols):
    width = cols // LANES * LANES
    rest = cols - width
    groups = width // rest
    return width, rest, groups, rows // groups


def pack(block, out):
    rows, cols = block.shape
    width, rest, groups, height = packing(rows, cols)
    out[:rows] = block[:, :width].astype(BF16)
    for g in range(groups):
        out[rows:, g * rest : (g + 1) * rest] = block[g * height : (g + 1) * height, width:].astype(BF16)


def copy_rows(panel, i, begin, ref, rows, width):
    step = math.gcd(math.gcd(rows, begin), 64)

    @pl.loop(0, rows // step)
    def _(k):
        at = pl.multiple_of(k * step, step)
        panel[i, pl.ds(begin + at, step), :width] = ref[pl.ds(at, step), :]


def fill(panel, refs, skip=0):
    half, cols = panel.shape[1:]
    rows = half // 2
    width, rest, groups, height = packing(rows, cols)
    total = rows + height
    at = skip * total
    for ref in refs:
        size = ref.shape[0]
        block, begin = divmod(at, total)
        i, base = divmod(block * rows, half)
        main = min(size, rows - begin)
        copy_rows(panel, i, base + begin, ref, main, width)
        if begin + size == total:
            for g in range(groups):
                low = base + g * height
                panel[i, low : low + height, width:] = ref[main:, g * rest : (g + 1) * rest]
        at += size


def pack_body(place, own, packed, copy):
    value = own[...]
    copy[...] = value
    pack(value.astype(F32), packed)


def chunk(z, far, size):
    return pl.ds(pl.multiple_of(lax.rem(z + far, RING) * size, 8), size)


DIMS = (((1,), (1,)), ((), ()))


def gram_body(place, own, *refs):
    *blocks, keep, send, panel, partner, rows, left = refs
    fill(panel, blocks)
    z, c = place[0], place[1]
    height = own.shape[0]
    panel[2, :height] = panel[0, height:]
    panel[2, height:] = panel[1, :height]
    left[0], left[1] = own[...], panel[1, height:]

    @pl.loop(0, 3)
    def _(i):
        rows[i] = lax.dot_general(left[jnp.where(i == 2, 1, 0)], panel[i], DIMS, preferred_element_type=F32)

    partner[...] = rows[2]
    split_units(z, c, rows, keep, send)


def split_units(z, c, rows, keep, send):
    size = keep.shape[1]

    @pl.loop(0, RING)
    def _(far):
        for side, out in ((c, keep), (1 - c, send)):
            out[far] = rows[side, chunk(z, far, size), :].astype(BF16)


def late_body(place, own, low, partner, top, bottom, keep, send, rows, panel):
    z, c = place[0], place[1]
    height = own.shape[0]
    fill(panel, [top, bottom])
    rows[0] = partner[...]
    rows[1, :, :height] = lax.dot_general(low[1, height:], panel[0, :height], DIMS, preferred_element_type=F32)
    rows[1, :, height:] = lax.dot_general(own[...], panel[0, :height], DIMS, preferred_element_type=F32)
    split_units(z, c, rows, keep, send)


def panel_body(place, low, *refs):
    *blocks, panel, high = refs
    fill(high, blocks)

    @pl.loop(0, 2)
    def _(i):
        panel[i] = low[i]
        panel[i + 2] = high[i]


def pair_body(place, low, low_other, high, high_other, *outs):
    size = low.shape[1]
    for d in range(RING):
        lower = (low[d].astype(F32) + low_other[d].astype(F32)).astype(BF16)
        upper = (high[d].astype(F32) + high_other[d].astype(F32)).astype(BF16)
        if d == FAR:
            outs[d][...] = lower
            outs[d + 1][...] = upper
        else:
            out = outs[d if d < FAR else d + 1]
            out[:size] = lower
            out[size:] = upper


def add(a, b):
    return (a.astype(F32) + b.astype(F32)).astype(BF16)


def ring_sum(place, part, up, down):
    size = up.shape[0]
    for step in range(FAR - 1, -1, -1):
        up = shift(up, "z", -1)
        down = shift(down, "z", 1)
        if step == 0:
            return call(sum_body, place, (part[0], up, down), [array(part[0].shape), array((size, up.shape[1]))])
        elif step == FAR - 1:
            one, two = part[step], part[RING - step]
            up = jnp.concatenate([add(one[:size], up), one[size:]], 0)
            down = jnp.concatenate([two[:size], add(two[size:], down)], 0)
        else:
            up, down = add(part[step], up), add(part[RING - step], down)


def sum_body(place, near, up, down, mine, ahead):
    size = ahead.shape[0]
    total = near[...].astype(F32) + up[...].astype(F32) + down[...].astype(F32)
    mine[...] = total.astype(BF16)
    ahead[...] = total[size:].astype(BF16)


def join_body(place, mine, across, same, cross, out):
    size, width = same.shape
    own = mine[...].astype(F32) + across[...].astype(F32)
    ahead = same[...].astype(F32) + cross[...].astype(F32)
    right = lax.broadcasted_iota(jnp.int32, (size, width), 1) >= width // 2
    out[:size] = own[:size].astype(BF16)
    out[size:] = jnp.where(right & (place[1] == 1), own[size:], ahead).astype(BF16)


def group_body(place, *refs):
    *pieces, out = refs
    for i, ref in enumerate(pieces):
        out[i] = ref[...]


def lay(gram, side, group, z):
    size = gram.shape[1] // RING

    @pl.loop(0, RING - 1)
    def _(i):
        where = chunk(z, i + jnp.where(i >= FAR, 1, 0), size)
        gram[side, where, :] = group[i, :size]
        gram[side + 2, where, :] = group[i, size:]

    @pl.loop(0, 2)
    def _(i):
        gram[side + 2 * i, chunk(z, FAR, size), :] = jnp.zeros((size, gram.shape[2]), BF16)


def own_rows_body(place, panel, group, gram, total):
    z, c = place[0], place[1]
    lay(gram, c, group, z)
    total[...] = jnp.zeros(total.shape, F32)

    @pl.loop(0, 2)
    def _(i):
        total[...] += jnp.dot(gram[c + 2 * i], panel[c + 2 * i], preferred_element_type=F32)


def other_rows_body(place, panel, group, before_gram, before, gram, total):
    z, side = place[0], 1 - place[1]
    lay(gram, side, group, z)

    @pl.loop(0, 2)
    def _(i):
        total[...] += jnp.dot(gram[side + 2 * i], panel[side + 2 * i], preferred_element_type=F32)


def update_body(place, own, panel, before_gram, before, mine, other, gram, w_high, w_low, total, acc):
    z, c = place[0], place[1]
    size = gram.shape[1] // RING
    where = chunk(z, FAR, size)
    for side, ref in ((c, mine), (1 - c, other)):
        gram[side, where, :] = ref[:size]
        gram[side + 2, where, :] = ref[size:]
    acc[...] = jnp.zeros(acc.shape, F32)

    @pl.loop(0, 4)
    def _(i):
        acc[...] += jnp.dot(gram[i, where, :], panel[i], preferred_element_type=F32)

    total[...] = before[...]
    total[where, :] = acc[...]
    w = coef_b * own[...].astype(F32) + coef_c * total[...]
    pack(w, w_high)
    w_low[...] = (w - w.astype(BF16).astype(F32)).astype(BF16)


def near_body(place, own, w_low, gram, *refs):
    *blocks, total, panel = refs
    rows = own.shape[0]
    fill(panel, blocks)
    panel[2, :rows] = w_low[...]
    panel[2, rows:] = jnp.zeros((rows, own.shape[1]), BF16)
    total[...] = coef_a * own[...].astype(F32)

    @pl.loop(0, 3)
    def _(i):
        total[...] += jnp.dot(gram[jnp.where(i == 2, 0, i)], panel[i], preferred_element_type=F32)


def side_body(place, before, gram, r11, r31, r20, total, panel):
    rows = total.shape[0]
    fill(panel, [r11, r31])
    fill(panel, [r20], 3)
    panel[1, :rows] = jnp.zeros((rows, total.shape[1]), BF16)
    total[...] = before[...]

    @pl.loop(0, 2)
    def _(i):
        total[...] += jnp.dot(gram[i + 2], panel[i], preferred_element_type=F32)


def far_body(place, before, gram, *refs):
    *pieces, out, panel = refs
    rows, cols = out.shape
    fill(panel, pieces)
    acc = before[...] + jnp.dot(gram[3][:, :rows], panel[0, :rows], preferred_element_type=F32)
    factor = 0.2 * math.sqrt(max(rows * PANEL, cols * math.prod(SIZES[n] for n in COL)))
    out[...] = (acc * factor).astype(BF16)


def newton_step(matrix):
    rows, cols = matrix.shape
    size = rows // RING
    place = jnp.stack([lax.axis_index("z"), lax.axis_index("c")]).astype(jnp.int32)
    width, _, _, height = packing(rows, cols)
    flat = array((rows + height, width))
    block = array((rows, cols))

    packed, own = call(pack_body, place, (matrix,), [flat, block], fixed=False)
    near = near_blocks(packed)
    r20 = halves_of(near[0], near[1])
    part = array((RING, size, 2 * rows))
    wide = array((4, rows, 2 * rows))
    sums = array((rows, cols), F32)
    work = 4 * rows * rows * cols

    def room(count, kind=BF16, width=cols):
        return pltpu.VMEM((count, 2 * rows, width), kind)

    pairs = pltpu.VMEM((2, rows, 2 * rows), F32)
    keep, send, low, partner = call(
        gram_body,
        place,
        (own, packed, *near),
        [part, part, array((3, 2 * rows, cols)), array((rows, 2 * rows), F32)],
        3 * work,
        [pltpu.VMEM((3, rows, 2 * rows), F32), pltpu.VMEM((2, rows, cols), BF16)],
    )
    halves = [keep, shift(send, "c", 1)]
    scratch = [pairs, room(1)]
    keep, send = call(late_body, place, (own, low, partner, *r20), [part, part], work, scratch)
    halves += [keep, shift(send, "c", 1)]
    r11 = shift(near[2], "x", 1)
    r31 = shift(near[2], "x", -1)
    r21 = jnp.concatenate(r20, 0)
    r21 = shift(r21, "yl", 1)
    panel = call(panel_body, place, (low, r11, r31, r21, *r20), array((4, 2 * rows, cols)), 0, [room(2)])
    one, two = array((size, 2 * rows)), array((2 * size, 2 * rows))
    parts = call(pair_body, place, halves, [two] * FAR + [one] * 2 + [two] * (FAR - 1))
    part = {d: parts[d if d < FAR else d + 1] for d in range(RING) if d != FAR}
    mine, ahead = ring_sum(place, part, parts[FAR], parts[FAR + 1])
    across = shift(mine, "yh", 1)
    same = shift(ahead, "yl", 1)
    cross = fetch(ahead, ("yl", "yh"), lambda y, h: (y + 1, h + 1))
    mine = call(join_body, place, (mine, across, same, cross), array(mine.shape))

    ring = {0: mine}
    up, down = mine, mine
    for step in range(1, FAR):
        up = shift(up, "z", 1)
        down = shift(down, "z", -1)
        ring[step], ring[RING - step] = up, down
    ends = [shift(up[:size], "z", 1)]
    ends.append(shift(down[size:], "z", -1))
    pieces = [ring[d] for d in range(RING) if d != FAR]
    group = call(group_body, place, pieces, array((RING - 1, 2 * size, 2 * rows)))
    ends = jnp.concatenate(ends, 0)

    other = shift(group, "c", 1)
    gram, total = call(own_rows_body, place, (panel, group), [wide, sums], 2 * work)
    gram, total = call(other_rows_body, place, (panel, other, gram, total), [wide, sums], 2 * work, alias={3: 0, 4: 1})
    gram, w_high, w_low = call(
        update_body,
        place,
        (own, panel, gram, total, ends, shift(ends, "c", 1)),
        [wide, flat, block],
        work // 2,
        [pltpu.VMEM((rows, cols), F32), pltpu.VMEM((size, cols), F32)],
        alias={3: 0},
    )

    near = near_blocks(w_high)
    _, r30, r01 = near
    r20 = shift(r30, "x", -1)
    r11 = shift(r01, "x", 1)
    r31 = shift(r30, "yl", 1)
    r20, r11, r31 = lax.optimization_barrier((r20, r11, r31))
    total = call(near_body, place, (own, w_low, gram, w_high, *near), sums, 3 * work, [room(3)])
    total = call(side_body, place, (total, gram, r11, r31, r20), sums, 2 * work, [room(2)])
    r21 = halves_of(r11, r31)
    return call(far_body, place, (total, gram, *r21), block, work // 2, [room(1)], home=True)


def solution(mesh):
    fine = Mesh(mesh.devices.reshape(tuple(SIZES.values())), AXES)
    return jax.shard_map(newton_step, mesh=fine, in_specs=(P(ROW, COL),), out_specs=P(ROW, COL), check_vma=False)
```
